512 devices in a mesh: cluster: 16 (over z), vector: 8 (over y, core), replica: 4 (over x).
Axes of the slice: x: 4, y: 4, z: 16, core: 2. Of those that a mesh axis runs over, the one named last changes fastest.
Arguments:
- samples: bfloat16 [128, 524288], P('vector', ('cluster', 'replica')), may hold values from -6 to 6
- leaf_basis_matrix: bfloat16 [32, 64, 8192], P(None, None, ('cluster', 'replica')), may hold values from -0.75 to 0.75
- transfer: bfloat16 [32, 32, 8192], P(None, None, ('cluster', 'replica')), may hold values from -0.75 to 0.75
- leaf_lists: int32 [4, 8192], P(None, ('cluster', 'replica')), may hold values from 0 to 8191, as said below
- leaf_coupling: bfloat16 [32, 32, 4, 8192], P(None, None, None, ('cluster', 'replica')), may hold values from -0.5 to 0.5
- parent_lists: int32 [4, 4096], P(None, ('cluster', 'replica')), may hold values from 0 to 4095, as said below
- parent_coupling: bfloat16 [32, 32, 4, 4096], P(None, None, None, ('cluster', 'replica')), may hold values from -0.5 to 0.5
- test_matrix: bfloat16 [128, 32], P('vector'), may hold values from -0.5 to 0.5
Outputs:
- product: bfloat16 [128, 524288], P('vector', ('cluster', 'replica'))
- new_basis: float32 [64, 32, 8192], P(None, None, ('cluster', 'replica'))
- fresh_transfer_sketch: float32 [32, 32, 8192], P(None, None, ('cluster', 'replica'))
The draws below stay inside these ranges and needn't reach their ends.
Inputs may be any that keep to these rules, and one draw needn't show every extreme that they name: `leaf_lists`: every source leaf lies within 128 leaves of its target leaf, and some source lies exactly 128 leaves away. `parent_lists`: every source parent lies within half of 128 parents of its target parent, and some source lies exactly that far away.
All inputs are finite; a program needn't handle non-finite values.
Results may differ from the reference program's by a relative error of at most 0.0062.
Values may be sent and summed in bfloat16 or wider, within the bound.
No kernel may reach another device: no remote copies, remote signals or barrier semaphores. Data moves between devices by JAX's collectives and lax.ppermute only.
A program may use at most 64 MiB of HBM per device.

```python
import jax
import jax.numpy as jnp
from jax import lax

P_SIZE = 64
R = 32
VEC = 128
LEAF_COUPLINGS = 4
K_PAR = 4
LEAF_DEV = 128
NLEAF = 8192
NPAR = 4096
NPTS = 524288


def near_lists(key, blocks, count, reach):
    targets = jnp.arange(count, dtype=jnp.int32)[None, :]
    offsets = jax.random.randint(key, (blocks, count), -reach, reach + 1, dtype=jnp.int32)
    sources = jnp.clip(targets + offsets, 0, count - 1)
    return sources.at[0, 0].set(reach)


def draw_leaf_lists(key, part):
    return near_lists(jax.random.fold_in(key, 11), LEAF_COUPLINGS, NLEAF, LEAF_DEV)


def draw_parent_lists(key, part):
    return near_lists(jax.random.fold_in(key, 23), K_PAR, NPAR, LEAF_DEV // 2)


def block_scale(stream_key, dims, pieces, least, largest):
    def one(position, blocks):
        draws = jax.random.uniform(jax.random.fold_in(jax.random.fold_in(stream_key, 6), position), (blocks,), jnp.float32, least / len(pieces), largest / len(pieces))
        return jnp.repeat(jnp.exp(draws), dims[position] // blocks).reshape((-1,) + (1,) * (len(dims) - position - 1))

    loudness = one(*pieces[0])
    for cut in pieces[1:]:
        loudness = loudness * one(*cut)
    return loudness


def scatter_about(rng, dims, scale, most, cuts=(), kind=jnp.bfloat16):
    drawn = scale * jax.random.normal(rng, dims, jnp.float32)
    if cuts:
        drawn = drawn * block_scale(rng, dims, cuts, -0.22, 0.18)
    return jnp.clip(drawn, -most, most).astype(kind)


def setup_inputs(seed: int = 0) -> dict:
    streams_of = jax.random.split(jax.random.key(seed), 9)
    return {
        "samples": scatter_about(streams_of[0], (VEC, NPTS), 1.0, 6.0, ((0, 8), (1, 64))),
        "leaf_basis_matrix": scatter_about(streams_of[1], (R, P_SIZE, NLEAF), P_SIZE ** -0.5, 0.75, ((2, 64),)),
        "transfer": scatter_about(streams_of[2], (R, R, NLEAF), (2 * R) ** -0.5, 0.75, ((2, 64),)),
        "leaf_lists": draw_leaf_lists(jax.random.fold_in(streams_of[8], 71), 0),
        "leaf_coupling": scatter_about(streams_of[4], (R, R, LEAF_COUPLINGS, NLEAF), (LEAF_COUPLINGS * R) ** -0.5, 0.5, ((3, 64),)),
        "parent_lists": draw_parent_lists(jax.random.fold_in(streams_of[8], 71), 0),
        "parent_coupling": scatter_about(streams_of[6], (R, R, K_PAR, NPAR), (K_PAR * R) ** -0.5, 0.5, ((3, 64),)),
        "test_matrix": scatter_about(streams_of[7], (VEC, R), VEC ** -0.5, 0.5, ((0, 8),)),
    }


def finish_basis(sketch, width):
    scale = lax.rsqrt(lax.optimization_barrier(jnp.mean(sketch * sketch, axis=0, keepdims=True)) + 1e-06)
    new_basis = sketch * scale
    fresh_transfer_sketch = jnp.einsum('pal,pbl->abl', new_basis, sketch, precision=lax.Precision.HIGHEST) / width
    return (new_basis, fresh_transfer_sketch)

def reference(samples, leaf_basis_matrix, transfer, leaf_lists, leaf_coupling, parent_lists, parent_coupling, test_matrix):
    rank, width, leaves = leaf_basis_matrix.shape
    vectors = samples.shape[0]
    each_leaf_amount = samples.reshape(vectors, leaves, width).astype(jnp.float32)
    leaf_coeff = jnp.einsum('rpl,vlp->rvl', leaf_basis_matrix.astype(jnp.float32), each_leaf_amount).astype(jnp.bfloat16)
    pairs = transfer.astype(jnp.float32).reshape(rank, rank, leaves // 2, 2)
    children = leaf_coeff.astype(jnp.float32).reshape(rank, vectors, leaves // 2, 2)
    parent_coeff = jnp.einsum('abqc,avqc->bvq', pairs, children).astype(jnp.bfloat16)
    leaf_src = leaf_coeff[:, :, leaf_lists].astype(jnp.float32)
    leaf_far = jnp.einsum('rskt,svkt->rvt', leaf_coupling.astype(jnp.float32), leaf_src)
    parent_src = parent_coeff[:, :, parent_lists].astype(jnp.float32)
    parent_far = jnp.einsum('rskq,svkq->rvq', parent_coupling.astype(jnp.float32), parent_src)
    descend = jnp.einsum('abqc,bvq->avqc', pairs, parent_far, precision=lax.Precision.HIGHEST)
    leaf_count_total = (leaf_far + descend.reshape(rank, vectors, leaves)).astype(jnp.bfloat16)
    product = jnp.einsum('etw,ebw->bwt', leaf_basis_matrix.astype(jnp.float32), leaf_count_total.astype(jnp.float32)).astype(jnp.bfloat16)
    sketch = jnp.einsum('vlp,vr->prl', product.astype(jnp.float32), test_matrix.astype(jnp.float32))
    new_basis, fresh_transfer_sketch = finish_basis(sketch, width)
    return (product.reshape(vectors, leaves * width), new_basis, fresh_transfer_sketch)
```

```python
import functools

import jax
import jax.numpy as jnp
from jax import lax
from jax.experimental import pallas as pl
from jax.experimental.pallas import tpu as pltpu
from jax.sharding import PartitionSpec as P

F32, BF16 = jnp.float32, jnp.bfloat16
HOPS = ("cluster", "replica")


def iota(shape, dim):
    return lax.broadcasted_iota(jnp.int32, shape, dim)


def picked(mask):
    return jnp.where(mask, 1.0, 0.0).astype(BF16)


def dot(a, b, contract=((1,), (0,))):
    return lax.dot_general(a, b, (contract, ((), ())), preferred_element_type=F32)


def widen(src, dst, step):
    tiles = step // 8

    def body(i, _):
        rows = src[pl.ds(pl.multiple_of(i * step, step), step), :].astype(F32)
        dst[pl.ds(i * tiles, tiles)] = rows.reshape(tiles, 8, rows.shape[-1])
        return 0

    lax.fori_loop(0, src.shape[0] // step, body, 0)


def lane_product(out, left, right, blocks, block, chunks, tile_of, right_of, start=None):
    wide = right.shape[-1]

    def outer(blk, _):
        first = [blk * block + i for i in range(block)]

        def inner(chunk, acc):
            acc = list(acc)
            tiles = [tile_of(o, chunk) for o in first]
            for c in range(8):
                term = right_of(chunk, c)
                for i in range(block):
                    acc[i] = acc[i] + left[tiles[i], c : c + 1, :] * term
            return tuple(acc)

        rows = out.shape[1]
        init = tuple(
            jnp.zeros((rows, wide), F32) if start is None else start[o] for o in first
        )
        acc = lax.fori_loop(0, chunks, inner, init)
        for i, o in enumerate(first):
            out[o] = acc[i]
        return 0

    lax.fori_loop(0, blocks, outer, 0)


def coeff_kernel(samples, basis, transfer, out, basis_w, transfer_w, xj, points, leaf, parent):
    vecs = samples.shape[0]
    widen(basis, basis_w, 64)
    widen(transfer, transfer_w, 64)
    for j in range(64):
        xj[pl.ds(j * vecs, vecs), :] = samples[:, 128 * j : 128 * (j + 1)].astype(F32)
    even = picked(iota((64, 128), 1) == 2 * iota((64, 128), 0))
    odd = picked(iota((64, 128), 1) == 2 * iota((64, 128), 0) + 1)
    for v in range(vecs):
        turned = xj[pl.ds(v, 64, stride=vecs), :].T
        both = dot(turned[:64].astype(BF16), even) + dot(turned[64:].astype(BF16), odd)
        points[:, v, :] = both
    lane_product(
        leaf, basis_w, points, 4, 8, 8,
        lambda r, chunk: r * 8 + chunk,
        lambda chunk, c: points[chunk * 8 + c],
    )
    rounded = leaf[...].astype(BF16)
    out[0:512, :] = rounded.reshape(512, 128)
    leaf[...] = rounded.astype(F32)

    def outer(blk, _):
        def inner(a, acc):
            src = leaf[a]
            return tuple(
                acc[i] + transfer_w[a * 4 + blk, i : i + 1, :] * src for i in range(8)
            )

        acc = lax.fori_loop(0, 32, inner, tuple(jnp.zeros((vecs, 128), F32) for _ in range(8)))
        for i in range(8):
            parent[blk * 8 + i] = acc[i] + pltpu.roll(acc[i], 127, 1)
        return 0

    lax.fori_loop(0, 4, outer, 0)
    low = picked(iota((128, 128), 0) == 2 * iota((128, 128), 1))
    high = picked(iota((128, 128), 0) == 2 * iota((128, 128), 1) - 128)
    sums = parent[...].reshape(512, 128).astype(BF16)
    out[512:768, :] = (dot(sums[0:256], low) + dot(sums[256:512], high)).astype(BF16)


def far_kernel(
    own, before, after, leaf_lists, parent_lists, transfer, test, leaf_coupling, parent_coupling,
    out, leaf_b, parent_b, coupling_w, parent_w, transfer_w, source, far, pfar, wide, sem,
):
    copies = [
        pltpu.make_async_copy(leaf_coupling, leaf_b, sem.at[0]),
        pltpu.make_async_copy(parent_coupling, parent_b, sem.at[1]),
    ]
    for copy in copies:
        copy.start()
    place = lax.axis_index("cluster") * lax.axis_size("replica") + lax.axis_index("replica")
    widen(transfer, transfer_w, 64)

    first = place * 64 - 64
    half = iota((128, 128), 0) // 64
    row = iota((128, 128), 0) % 64
    twice = picked(iota((64, 128), 0) == iota((64, 128), 1) % 64)
    packed = jnp.concatenate([before[512:768], own[512:768], after[512:768]], axis=1)
    for k in range(4):
        index = jnp.broadcast_to(parent_lists[k : k + 1, :] - first, (64, 64))
        cols = []
        for h in range(2):
            parts = []
            for m in range(3):
                hit = dot(picked(iota((64, 64), 0) + 64 * m == index), twice).astype(BF16)
                none = jnp.zeros((64, 128), BF16)
                parts += [hit, none] if h == 0 else [none, hit]
            cols.append(jnp.concatenate(parts, axis=0))
        for h in range(2):
            got = dot(packed, cols[h])
            source[k, 16 * h : 16 * (h + 1)] = got.reshape(16, 16, 128)

    copies[1].wait()

    def pack(i, _):
        low = parent_b[pl.ds(pl.multiple_of(i * 64, 64), 64), :].astype(F32)
        high = parent_b[pl.ds(pl.multiple_of(2048 + i * 64, 64), 64), :].astype(F32)
        both = jnp.concatenate([low, high], axis=1)
        parent_w[pl.ds(i * 8, 8)] = both.reshape(8, 8, 128)
        return 0

    lax.fori_loop(0, 32, pack, 0)
    lane_product(
        pfar, parent_w, source, 2, 8, 16,
        lambda r, chunk: r * 16 + chunk,
        lambda chunk, c: source[c % 4, chunk * 2 + c // 4],
    )
    lane = iota((256, 128), 1) // 2
    flat = pfar[...].reshape(256, 128)
    wide[0:16] = jnp.take_along_axis(flat, lane, axis=1).reshape(16, 16, 128)
    wide[16:32] = jnp.take_along_axis(flat, lane + 64, axis=1).reshape(16, 16, 128)

    first = place * 128 - 128
    rows = jnp.concatenate([before[0:512], own[0:512], after[0:512]], axis=1)
    for k in range(4):
        index = jnp.broadcast_to(leaf_lists[k : k + 1, :] - first, (384, 128))
        source[k] = dot(rows, picked(iota((384, 128), 0) == index)).reshape(32, 16, 128)
    copies[0].wait()
    widen(leaf_b, coupling_w, 64)
    lane_product(
        far, coupling_w, source, 4, 8, 16,
        lambda r, chunk: r * 16 + chunk,
        lambda chunk, c: source[c % 4, chunk * 2 + c // 4],
    )
    lane_product(
        far, transfer_w, wide, 4, 8, 4,
        lambda a, chunk: a * 4 + chunk,
        lambda chunk, c: wide[chunk * 8 + c],
        start=far,
    )
    out[0:512, :] = far[...].reshape(512, 128).astype(BF16)
    pad = jnp.zeros((16, 128 - 32), BF16)
    out[512:528, :] = jnp.concatenate([test[...], pad], axis=1)


def product_kernel(total, basis, out, basis_w, total_w, grid, turned):
    widen(basis, basis_w, 64)
    total_w[...] = total[0:512, :].astype(F32).reshape(32, 16, 128)

    def outer(blk, _):
        def inner(a, acc):
            src = total_w[a]
            return tuple(acc[i] + basis_w[a * 8 + blk, i : i + 1, :] * src for i in range(8))

        acc = lax.fori_loop(0, 32, inner, tuple(jnp.zeros((16, 128), F32) for _ in range(8)))
        for i in range(8):
            grid[blk * 8 + i] = acc[i]
        return 0

    lax.fori_loop(0, 8, outer, 0)
    even = picked(iota((64, 128), 1) == 2 * iota((64, 128), 0))
    odd = picked(iota((64, 128), 1) == 2 * iota((64, 128), 0) + 1)
    none = jnp.zeros((64, 128), BF16)
    for v in range(16):
        mine = grid[:, v, :].astype(BF16)
        turned[:, v, :] = dot(even, jnp.concatenate([mine, none], axis=0), ((1,), (1,))) + dot(
            odd, jnp.concatenate([none, mine], axis=0), ((1,), (1,))
        )
    for j in range(64):
        out[:, 128 * j : 128 * (j + 1)] = turned[j].astype(BF16)


def basis_kernel(totals, basis, new_basis, fresh, basis_w, compressed, sketch, scale_w):
    groups = totals.shape[0]
    widen(basis, basis_w, 64)
    tests = jnp.concatenate([totals[g, 512:528, :] for g in range(groups)], axis=0)
    across = tests.astype(F32).T[0:32].astype(BF16)
    for a in range(32):
        rows = jnp.concatenate([totals[g, 16 * a : 16 * (a + 1), :] for g in range(groups)], axis=0)
        compressed[a] = dot(across, rows)

    def outer(blk, square):
        def inner(a, acc):
            src = compressed[a]
            return tuple(acc[i] + basis_w[a * 8 + blk, i : i + 1, :] * src for i in range(8))

        acc = lax.fori_loop(0, 32, inner, tuple(jnp.zeros((32, 128), F32) for _ in range(8)))
        for i in range(8):
            sketch[blk * 8 + i] = acc[i]
            square = square + acc[i] * acc[i]
        return square

    square = lax.fori_loop(0, 8, outer, jnp.zeros((32, 128), F32))
    scale = lax.rsqrt(square / 64 + 1e-06)
    scale_w[...] = scale

    def scaled(p, _):
        new_basis[p] = sketch[p] * scale_w[...]
        return 0

    lax.fori_loop(0, 64, scaled, 0)

    def gram(blk, _):
        base = pl.multiple_of(blk * 8, 8)

        def inner(p, acc):
            src = sketch[p]
            mine = new_basis.at[p]
            return tuple(acc[i] + mine[pl.ds(base + i, 1), :] * src for i in range(8))

        acc = lax.fori_loop(0, 64, inner, tuple(jnp.zeros((32, 128), F32) for _ in range(8)))
        for i in range(8):
            fresh[blk * 8 + i] = acc[i] * (1.0 / 64)
        return 0

    lax.fori_loop(0, 4, gram, 0)


def shards(
    samples, leaf_basis_matrix, transfer, leaf_lists, leaf_coupling, parent_lists,
    parent_coupling, test_matrix,
):
    basis = leaf_basis_matrix.reshape(2048, 128)
    moves = transfer.reshape(1024, 128)
    near = leaf_coupling.reshape(4096, 128)
    above = parent_coupling.reshape(4096, 64)
    vmem = pl.BlockSpec(memory_space=pltpu.VMEM)
    anywhere = pl.BlockSpec(memory_space=pl.ANY)

    coeff = pl.pallas_call(
        coeff_kernel,
        out_shape=jax.ShapeDtypeStruct((768, 128), BF16),
        in_specs=[vmem] * 3,
        out_specs=vmem,
        scratch_shapes=[
            pltpu.VMEM((256, 8, 128), F32),
            pltpu.VMEM((128, 8, 128), F32),
            pltpu.VMEM((1024, 128), F32),
            pltpu.VMEM((64, 16, 128), F32),
            pltpu.VMEM((32, 16, 128), F32),
            pltpu.VMEM((32, 16, 128), F32),
        ],
        name="coeff",
    )(samples, basis, moves)

    peers = lax.axis_size("cluster") * lax.axis_size("replica")
    up = [(i, (i + 1) % peers) for i in range(peers)]
    before = lax.ppermute(coeff, HOPS, up)
    after = lax.ppermute(coeff, HOPS, [(b, a) for a, b in up])

    total = pl.pallas_call(
        far_kernel,
        out_shape=jax.ShapeDtypeStruct((528, 128), BF16),
        in_specs=[vmem] * 7 + [anywhere] * 2,
        out_specs=vmem,
        scratch_shapes=[
            pltpu.VMEM((4096, 128), BF16),
            pltpu.VMEM((4096, 64), BF16),
            pltpu.VMEM((512, 8, 128), F32),
            pltpu.VMEM((256, 8, 128), F32),
            pltpu.VMEM((128, 8, 128), F32),
            pltpu.VMEM((4, 32, 16, 128), F32),
            pltpu.VMEM((32, 16, 128), F32),
            pltpu.VMEM((16, 16, 128), F32),
            pltpu.VMEM((32, 16, 128), F32),
            pltpu.SemaphoreType.DMA((2,)),
        ],
        name="far",
    )(coeff, before, after, leaf_lists, parent_lists, moves, test_matrix, near, above)

    groups = lax.axis_size("vector")
    totals = lax.all_to_all(
        jnp.broadcast_to(total[None], (groups, *total.shape)), "vector", 0, 0, tiled=True
    )

    product = pl.pallas_call(
        product_kernel,
        out_shape=jax.ShapeDtypeStruct((16, 8192), BF16),
        in_specs=[vmem] * 2,
        out_specs=vmem,
        scratch_shapes=[
            pltpu.VMEM((256, 8, 128), F32),
            pltpu.VMEM((32, 16, 128), F32),
            pltpu.VMEM((64, 16, 128), F32),
            pltpu.VMEM((64, 16, 128), F32),
        ],
        cost_estimate=pl.CostEstimate(flops=10**7, bytes_accessed=10**6, transcendentals=0),
        name="product",
    )(total, basis)

    new_basis, fresh = pl.pallas_call(
        basis_kernel,
        out_shape=(
            jax.ShapeDtypeStruct((64, 32, 128), F32),
            jax.ShapeDtypeStruct((32, 32, 128), F32),
        ),
        in_specs=[vmem] * 2,
        out_specs=(vmem, vmem),
        scratch_shapes=[
            pltpu.VMEM((256, 8, 128), F32),
            pltpu.VMEM((32, 32, 128), F32),
            pltpu.VMEM((64, 32, 128), F32),
            pltpu.VMEM((32, 128), F32),
        ],
        name="basis",
    )(totals, basis)
    return product, new_basis, fresh


def solution(mesh):
    placed = (
        P("vector", HOPS),
        P(None, None, HOPS),
        P(None, None, HOPS),
        P(None, HOPS),
        P(None, None, None, HOPS),
        P(None, HOPS),
        P(None, None, None, HOPS),
        P("vector", None),
    )
    return jax.shard_map(
        shards,
        mesh=mesh,
        in_specs=placed,
        out_specs=(P("vector", HOPS), P(None, None, HOPS), P(None, None, HOPS)),
        check_vma=False,
    )
```

```python
import jax
import jax.numpy as jnp
from jax import lax
from jax.experimental import pallas as pl
from jax.experimental.pallas import tpu as pltpu
from jax.sharding import PartitionSpec as P

F32, BF16 = jnp.float32, jnp.bfloat16
HOPS = ("cluster", "replica")


def iota(shape, dim):
    return lax.broadcasted_iota(jnp.int32, shape, dim)


def picked(mask):
    return jnp.where(mask, 1.0, 0.0).astype(BF16)


def dot(a, b, contract=((1,), (0,))):
    return lax.dot_general(a, b, (contract, ((), ())), preferred_element_type=F32)


def widen(src, dst, step=128):
    tiles = step // 8

    def body(i, _):
        rows = src[pl.ds(pl.multiple_of(i * step, step), step), :].astype(F32)
        dst[pl.ds(i * tiles, tiles)] = rows.reshape(tiles, 8, rows.shape[-1])
        return 0

    lax.fori_loop(0, src.shape[0] // step, body, 0)


def weighted(block, steps, unroll, weight, term, init):
    def body(group, acc):
        acc = list(acc)
        for u in range(unroll):
            src = term(group, u)
            for i in range(block):
                acc[i] = acc[i] + weight(i, group, u) * src
        return tuple(acc)

    return lax.fori_loop(0, steps // unroll, body, tuple(init))


def lane_product(out, left, right_of, blocks, chunks, per, tile_of, start=None, block=8):
    rows, wide = out.shape[1:]

    def outer(blk, _):
        first = [blk * block + i for i in range(block)]
        init = [jnp.zeros((rows, wide), F32) if start is None else start[o] for o in first]

        def weight(i, group, u):
            c = u % 8
            return left[tile_of(first[i], group * per + u // 8), c : c + 1, :]

        acc = weighted(
            block, chunks * 8, per * 8, weight,
            lambda group, u: right_of(group * per + u // 8, u % 8), init,
        )
        for i, o in enumerate(first):
            out[o] = acc[i]
        return 0

    lax.fori_loop(0, blocks, outer, 0)


def fetched(pairs, sem):
    copies = [pltpu.make_async_copy(a, b, sem.at[i]) for i, (a, b) in enumerate(pairs)]
    for copy in copies:
        copy.start()
    return copies


def coeff_kernel(
    samples_at, basis_at, transfer_at, out,
    samples, basis, transfer, basis_w, transfer_w, xj, points, leaf, parent, sem,
):
    copies = fetched(
        [(samples_at, samples), (basis_at, basis), (transfer_at, transfer)], sem
    )
    vecs = samples.shape[0]
    even = picked(iota((64, 128), 1) == 2 * iota((64, 128), 0))
    odd = picked(iota((64, 128), 1) == 2 * iota((64, 128), 0) + 1)
    copies[0].wait()
    for j in range(64):
        xj[pl.ds(j * vecs, vecs), :] = samples[:, 128 * j : 128 * (j + 1)].astype(F32)
    for v in range(vecs):
        turned = xj[pl.ds(v, 64, stride=vecs), :].T
        both = dot(turned[:64].astype(BF16), even) + dot(turned[64:].astype(BF16), odd)
        points[:, v, :] = both
    copies[1].wait()
    widen(basis, basis_w)
    lane_product(
        leaf, basis_w, lambda chunk, c: points[chunk * 8 + c], 4, 8, 4,
        lambda r, chunk: r * 8 + chunk,
    )
    rounded = leaf[...].astype(BF16)
    out[0:512, :] = rounded.reshape(512, 128)
    leaf[...] = rounded.astype(F32)
    copies[2].wait()
    widen(transfer, transfer_w)

    def outer(blk, _):
        acc = weighted(
            8, 32, 16,
            lambda i, group, u: transfer_w[(group * 16 + u) * 4 + blk, i : i + 1, :],
            lambda group, u: leaf[group * 16 + u],
            [jnp.zeros((vecs, 128), F32)] * 8,
        )
        for i in range(8):
            parent[blk * 8 + i] = acc[i] + pltpu.roll(acc[i], 127, 1)
        return 0

    lax.fori_loop(0, 4, outer, 0)
    low = picked(iota((128, 128), 0) == 2 * iota((128, 128), 1))
    high = picked(iota((128, 128), 0) == 2 * iota((128, 128), 1) - 128)
    sums = parent[...].reshape(512, 128).astype(BF16)
    out[512:768, :] = (dot(sums[0:256], low) + dot(sums[256:512], high)).astype(BF16)


def far_kernel(
    own_at, before_at, after_at, transfer_at, leaf_at, parent_at, leaf_lists, parent_lists, test,
    out, own, before, after, transfer, leaf_b, parent_b,
    coupling_w, parent_w, transfer_w, source, far, pfar, wide, payload, sem, sent,
):
    copies = fetched(
        [
            (own_at, own), (before_at, before), (after_at, after),
            (parent_at, parent_b), (leaf_at, leaf_b), (transfer_at, transfer),
        ],
        sem,
    )
    place = lax.axis_index("cluster") * lax.axis_size("replica") + lax.axis_index("replica")

    first = place * 64 - 64
    twice = picked(iota((64, 128), 0) == iota((64, 128), 1) % 64)
    none = jnp.zeros((64, 128), BF16)
    for copy in copies[:3]:
        copy.wait()
    packed = jnp.concatenate([before[512:768], own[512:768], after[512:768]], axis=1)
    for k in range(4):
        index = jnp.broadcast_to(parent_lists[k : k + 1, :] - first, (64, 64))
        hits = [
            dot(picked(iota((64, 64), 0) + 64 * m == index), twice).astype(BF16) for m in range(3)
        ]
        for h in range(2):
            parts = [part for hit in hits for part in ((hit, none) if h == 0 else (none, hit))]
            got = dot(packed, jnp.concatenate(parts, axis=0))
            source[k, 16 * h : 16 * (h + 1)] = got.reshape(16, 16, 128)

    copies[3].wait()

    def pack(i, _):
        low = parent_b[pl.ds(pl.multiple_of(i * 128, 128), 128), :].astype(F32)
        high = parent_b[pl.ds(pl.multiple_of(2048 + i * 128, 128), 128), :].astype(F32)
        both = jnp.concatenate([low, high], axis=1)
        parent_w[pl.ds(i * 16, 16)] = both.reshape(16, 8, 128)
        return 0

    lax.fori_loop(0, 16, pack, 0)
    lane_product(
        pfar, parent_w, lambda chunk, c: source[c % 4, chunk * 2 + c // 4], 2, 16, 4,
        lambda r, chunk: r * 16 + chunk,
    )
    lane = iota((256, 128), 1) // 2
    flat = pfar[...].reshape(256, 128)
    wide[0:16] = jnp.take_along_axis(flat, lane, axis=1).reshape(16, 16, 128)
    wide[16:32] = jnp.take_along_axis(flat, lane + 64, axis=1).reshape(16, 16, 128)

    first = place * 128 - 128
    rows = jnp.concatenate([before[0:512], own[0:512], after[0:512]], axis=1)
    for k in range(4):
        index = jnp.broadcast_to(leaf_lists[k : k + 1, :] - first, (384, 128))
        source[k] = dot(rows, picked(iota((384, 128), 0) == index)).reshape(32, 16, 128)
    copies[4].wait()
    widen(leaf_b, coupling_w)
    lane_product(
        far, coupling_w, lambda chunk, c: source[c % 4, chunk * 2 + c // 4], 4, 16, 4,
        lambda r, chunk: r * 16 + chunk,
    )
    copies[5].wait()
    widen(transfer, transfer_w)
    lane_product(
        far, transfer_w, lambda chunk, c: wide[chunk * 8 + c], 4, 4, 4,
        lambda a, chunk: a * 4 + chunk, start=far,
    )
    payload[0:512, :] = far[...].reshape(512, 128).astype(BF16)
    pad = jnp.zeros((16, 128 - 32), BF16)
    payload[512:528, :] = jnp.concatenate([test[...], pad], axis=1)
    for copy in fetched([(payload, out.at[i]) for i in range(out.shape[0])], sent):
        copy.wait()


def product_kernel(total_at, basis_at, out, total, basis, basis_w, total_w, grid, turned, sem):
    copies = fetched([(total_at.at[0], total), (basis_at, basis)], sem)
    for copy in copies:
        copy.wait()
    widen(basis, basis_w)
    total_w[...] = total[0:512, :].astype(F32).reshape(32, 16, 128)

    def outer(blk, _):
        acc = weighted(
            8, 32, 16,
            lambda i, group, u: basis_w[(group * 16 + u) * 8 + blk, i : i + 1, :],
            lambda group, u: total_w[group * 16 + u],
            [jnp.zeros((16, 128), F32)] * 8,
        )
        for i in range(8):
            grid[blk * 8 + i] = acc[i]
        return 0

    lax.fori_loop(0, 8, outer, 0)
    even = picked(iota((64, 128), 1) == 2 * iota((64, 128), 0))
    odd = picked(iota((64, 128), 1) == 2 * iota((64, 128), 0) + 1)
    none = jnp.zeros((64, 128), BF16)
    for v in range(16):
        mine = grid[:, v, :].astype(BF16)
        turned[:, v, :] = dot(even, jnp.concatenate([mine, none], axis=0), ((1,), (1,))) + dot(
            odd, jnp.concatenate([none, mine], axis=0), ((1,), (1,))
        )
    for j in range(64):
        out[:, 128 * j : 128 * (j + 1)] = turned[j].astype(BF16)


def basis_kernel(
    mine_at, theirs_at, basis_at, new_at, fresh_at,
    totals, basis, basis_w, compressed, sketch, scale_w, gram, new_basis, fresh, sem, sent,
):
    groups = totals.shape[0]
    half = mine_at.shape[0]
    copies = fetched(
        [(basis_at, basis), (mine_at, totals.at[0:half]), (theirs_at, totals.at[half:groups])], sem
    )
    copies[0].wait()
    widen(basis, basis_w)
    for copy in copies[1:]:
        copy.wait()
    tests = jnp.concatenate([totals[g, 512:528, :] for g in range(groups)], axis=0)
    across = tests.astype(F32).T[0:32].astype(BF16)
    for a in range(32):
        rows = jnp.concatenate([totals[g, 16 * a : 16 * (a + 1), :] for g in range(groups)], axis=0)
        compressed[a] = dot(across, rows)

    scale_w[...] = jnp.zeros((32, 128), F32)

    def outer(blk, _):
        acc = weighted(
            8, 32, 16,
            lambda i, group, u: basis_w[(group * 16 + u) * 8 + blk, i : i + 1, :],
            lambda group, u: compressed[group * 16 + u],
            [jnp.zeros((32, 128), F32)] * 8,
        )
        square = scale_w[...]
        for i in range(8):
            sketch[blk * 8 + i] = acc[i]
            square = square + acc[i] * acc[i]
        scale_w[...] = square
        return 0

    lax.fori_loop(0, 8, outer, 0)
    scale_w[...] = lax.rsqrt(scale_w[...] / 64 + 1e-06)

    def scaled(group, _):
        scale = scale_w[...]
        for u in range(8):
            new_basis[group * 8 + u] = sketch[group * 8 + u] * scale
        return 0

    lax.fori_loop(0, 8, scaled, 0)
    first = fetched([(new_basis, new_at)], sent)

    for tile in range(4):
        low = 8 * tile
        acc = weighted(
            8, 64, 16,
            lambda i, group, u: sketch[group * 16 + u, low + i : low + i + 1, :],
            lambda group, u: sketch[group * 16 + u, low:32, :],
            [jnp.zeros((32 - low, 128), F32)] * 8,
        )
        for i in range(8):
            gram[(low + i) * 32 + low : (low + i) * 32 + 32, :] = acc[i]
    for a in range(32):
        row = scale_w[a : a + 1, :] * (1.0 / 64)
        low = a // 8 * 8
        fresh[a, low:32, :] = gram[a * 32 + low : a * 32 + 32, :] * row
        for b in range(0, low, 8):
            fresh[a, b : b + 8, :] = gram[pl.ds(b * 32 + a, 8, stride=32), :] * row
    second = pltpu.make_async_copy(fresh, fresh_at, sent.at[1])
    second.start()
    first[0].wait()
    second.wait()


def shards(
    samples, leaf_basis_matrix, transfer, leaf_lists, leaf_coupling, parent_lists,
    parent_coupling, test_matrix,
):
    basis = leaf_basis_matrix.reshape(2048, 128)
    moves = transfer.reshape(1024, 128)
    near = leaf_coupling.reshape(4096, 128)
    above = parent_coupling.reshape(4096, 64)
    vmem = pl.BlockSpec(memory_space=pltpu.VMEM)
    anywhere = pl.BlockSpec(memory_space=pl.ANY)

    coeff = pl.pallas_call(
        coeff_kernel,
        out_shape=jax.ShapeDtypeStruct((768, 128), BF16),
        in_specs=[anywhere] * 3,
        out_specs=vmem,
        scratch_shapes=[
            pltpu.VMEM((16, 8192), BF16),
            pltpu.VMEM((2048, 128), BF16),
            pltpu.VMEM((1024, 128), BF16),
            pltpu.VMEM((256, 8, 128), F32),
            pltpu.VMEM((128, 8, 128), F32),
            pltpu.VMEM((1024, 128), F32),
            pltpu.VMEM((64, 16, 128), F32),
            pltpu.VMEM((32, 16, 128), F32),
            pltpu.VMEM((32, 16, 128), F32),
            pltpu.SemaphoreType.DMA((3,)),
        ],
        name="coeff",
    )(samples, basis, moves)

    peers = lax.axis_size("cluster") * lax.axis_size("replica")
    up = [(i, i + 1) for i in range(peers - 1)]
    before = lax.ppermute(coeff, HOPS, up)
    after = lax.ppermute(coeff, HOPS, [(b, a) for a, b in up])

    groups = lax.axis_size("vector")
    half = groups // 2
    total = pl.pallas_call(
        far_kernel,
        out_shape=jax.ShapeDtypeStruct((half, 528, 128), BF16),
        in_specs=[anywhere] * 6 + [vmem] * 3,
        out_specs=anywhere,
        scratch_shapes=[
            pltpu.VMEM((768, 128), BF16),
            pltpu.VMEM((768, 128), BF16),
            pltpu.VMEM((768, 128), BF16),
            pltpu.VMEM((1024, 128), BF16),
            pltpu.VMEM((4096, 128), BF16),
            pltpu.VMEM((4096, 64), BF16),
            pltpu.VMEM((512, 8, 128), F32),
            pltpu.VMEM((256, 8, 128), F32),
            pltpu.VMEM((128, 8, 128), F32),
            pltpu.VMEM((4, 32, 16, 128), F32),
            pltpu.VMEM((32, 16, 128), F32),
            pltpu.VMEM((16, 16, 128), F32),
            pltpu.VMEM((32, 16, 128), F32),
            pltpu.VMEM((528, 128), BF16),
            pltpu.SemaphoreType.DMA((6,)),
            pltpu.SemaphoreType.DMA((half,)),
        ],
        name="far",
    )(coeff, before, after, moves, near, above, leaf_lists, parent_lists, test_matrix)

    cores = [[2 * y + core for y in range(half)] for core in range(2)]
    mine = lax.all_to_all(total, "vector", 0, 0, tiled=True, axis_index_groups=cores)
    theirs = lax.ppermute(mine, "vector", [(i, i ^ 1) for i in range(groups)])

    product = pl.pallas_call(
        product_kernel,
        out_shape=jax.ShapeDtypeStruct((16, 8192), BF16),
        in_specs=[anywhere] * 2,
        out_specs=vmem,
        scratch_shapes=[
            pltpu.VMEM((528, 128), BF16),
            pltpu.VMEM((2048, 128), BF16),
            pltpu.VMEM((256, 8, 128), F32),
            pltpu.VMEM((32, 16, 128), F32),
            pltpu.VMEM((64, 16, 128), F32),
            pltpu.VMEM((64, 16, 128), F32),
            pltpu.SemaphoreType.DMA((2,)),
        ],
        cost_estimate=pl.CostEstimate(flops=10**7, bytes_accessed=10**6, transcendentals=0),
        name="product",
    )(total, basis)

    new_basis, fresh = pl.pallas_call(
        basis_kernel,
        out_shape=(
            jax.ShapeDtypeStruct((64, 32, 128), F32),
            jax.ShapeDtypeStruct((32, 32, 128), F32),
        ),
        in_specs=[anywhere] * 3,
        out_specs=(anywhere, anywhere),
        scratch_shapes=[
            pltpu.VMEM((groups, 528, 128), BF16),
            pltpu.VMEM((2048, 128), BF16),
            pltpu.VMEM((256, 8, 128), F32),
            pltpu.VMEM((32, 32, 128), F32),
            pltpu.VMEM((64, 32, 128), F32),
            pltpu.VMEM((32, 128), F32),
            pltpu.VMEM((1024, 128), F32),
            pltpu.VMEM((64, 32, 128), F32),
            pltpu.VMEM((32, 32, 128), F32),
            pltpu.SemaphoreType.DMA((3,)),
            pltpu.SemaphoreType.DMA((2,)),
        ],
        name="basis",
    )(mine, theirs, basis)
    return product, new_basis, fresh


def solution(mesh):
    placed = (
        P("vector", HOPS),
        P(None, None, HOPS),
        P(None, None, HOPS),
        P(None, HOPS),
        P(None, None, None, HOPS),
        P(None, HOPS),
        P(None, None, None, HOPS),
        P("vector", None),
    )
    return jax.shard_map(
        shards,
        mesh=mesh,
        in_specs=placed,
        out_specs=(P("vector", HOPS), P(None, None, HOPS), P(None, None, HOPS)),
        check_vma=False,
    )
```

```python
import jax
import jax.numpy as jnp
from jax import lax
from jax.experimental import pallas as pl
from jax.experimental.pallas import tpu as pltpu
from jax.sharding import PartitionSpec as P

F32, BF16 = jnp.float32, jnp.bfloat16
HOPS = ("cluster", "replica")


def iota(shape, dim):
    return lax.broadcasted_iota(jnp.int32, shape, dim)


def picked(mask):
    return jnp.where(mask, 1.0, 0.0).astype(BF16)


def dot(a, b, contract=((1,), (0,))):
    return lax.dot_general(a, b, (contract, ((), ())), preferred_element_type=F32)


def widen(src, dst, step=128):
    tiles = step // 8

    def body(i, _):
        rows = src[pl.ds(pl.multiple_of(i * step, step), step), :].astype(F32)
        dst[pl.ds(i * tiles, tiles)] = rows.reshape(tiles, 8, rows.shape[-1])
        return 0

    lax.fori_loop(0, src.shape[0] // step, body, 0)


def weighted(block, steps, unroll, weight, term, init):
    def body(group, acc):
        acc = list(acc)
        for u in range(unroll):
            src = term(group, u)
            for i in range(block):
                acc[i] = acc[i] + weight(i, group, u) * src
        return tuple(acc)

    return lax.fori_loop(0, steps // unroll, body, tuple(init))


def lane_product(out, left, right_of, blocks, chunks, per, tile_of, start=None, block=8):
    rows, wide = out.shape[1:]

    def outer(blk, _):
        first = [blk * block + i for i in range(block)]
        init = [jnp.zeros((rows, wide), F32) if start is None else start[o] for o in first]

        def weight(i, group, u):
            c = u % 8
            return left[tile_of(first[i], group * per + u // 8), c : c + 1, :]

        acc = weighted(
            block, chunks * 8, per * 8, weight,
            lambda group, u: right_of(group * per + u // 8, u % 8), init,
        )
        for i, o in enumerate(first):
            out[o] = acc[i]
        return 0

    lax.fori_loop(0, blocks, outer, 0)


def fetched(pairs, sem):
    copies = [pltpu.make_async_copy(a, b, sem.at[i]) for i, (a, b) in enumerate(pairs)]
    for copy in copies:
        copy.start()
    return copies


def coeff_kernel(
    samples_at, basis_at, transfer_at, out,
    samples, basis, transfer, basis_w, transfer_w, xj, points, leaf, parent, sem,
):
    copies = fetched(
        [(samples_at, samples), (basis_at, basis), (transfer_at, transfer)], sem
    )
    vecs = samples.shape[0]
    even = picked(iota((64, 128), 1) == 2 * iota((64, 128), 0))
    odd = picked(iota((64, 128), 1) == 2 * iota((64, 128), 0) + 1)
    copies[0].wait()
    for j in range(64):
        xj[pl.ds(j * vecs, vecs), :] = samples[:, 128 * j : 128 * (j + 1)].astype(F32)
    for v in range(vecs):
        turned = xj[pl.ds(v, 64, stride=vecs), :].T
        both = dot(turned[:64].astype(BF16), even) + dot(turned[64:].astype(BF16), odd)
        points[:, v, :] = both
    copies[1].wait()
    widen(basis, basis_w)
    lane_product(
        leaf, basis_w, lambda chunk, c: points[chunk * 8 + c], 4, 8, 4,
        lambda r, chunk: r * 8 + chunk,
    )
    rounded = leaf[...].astype(BF16)
    out[0:512, :] = rounded.reshape(512, 128)
    leaf[...] = rounded.astype(F32)
    copies[2].wait()
    widen(transfer, transfer_w)

    def outer(blk, _):
        acc = weighted(
            8, 32, 16,
            lambda i, group, u: transfer_w[(group * 16 + u) * 4 + blk, i : i + 1, :],
            lambda group, u: leaf[group * 16 + u],
            [jnp.zeros((vecs, 128), F32)] * 8,
        )
        for i in range(8):
            parent[blk * 8 + i] = acc[i] + pltpu.roll(acc[i], 127, 1)
        return 0

    lax.fori_loop(0, 4, outer, 0)
    low = picked(iota((128, 128), 0) == 2 * iota((128, 128), 1))
    high = picked(iota((128, 128), 0) == 2 * iota((128, 128), 1) - 128)
    sums = parent[...].reshape(512, 128).astype(BF16)
    out[512:768, :] = (dot(sums[0:256], low) + dot(sums[256:512], high)).astype(BF16)


def far_kernel(
    own_at, before_at, after_at, transfer_at, leaf_at, parent_at, leaf_lists, parent_lists, test,
    out, own, before, after, transfer, leaf_b, parent_b,
    coupling_w, parent_w, transfer_w, source, far, pfar, wide, payload, sem, sent,
):
    copies = fetched(
        [
            (own_at, own), (before_at, before), (after_at, after),
            (parent_at, parent_b), (leaf_at, leaf_b), (transfer_at, transfer),
        ],
        sem,
    )
    place = lax.axis_index("cluster") * lax.axis_size("replica") + lax.axis_index("replica")

    first = place * 64 - 64
    twice = picked(iota((64, 128), 0) == iota((64, 128), 1) % 64)
    none = jnp.zeros((64, 128), BF16)
    for copy in copies[:3]:
        copy.wait()
    packed = jnp.concatenate([before[512:768], own[512:768], after[512:768]], axis=1)
    for k in range(4):
        index = jnp.broadcast_to(parent_lists[k : k + 1, :] - first, (64, 64))
        hits = [
            dot(picked(iota((64, 64), 0) + 64 * m == index), twice).astype(BF16) for m in range(3)
        ]
        for h in range(2):
            parts = [part for hit in hits for part in ((hit, none) if h == 0 else (none, hit))]
            got = dot(packed, jnp.concatenate(parts, axis=0))
            source[k, 16 * h : 16 * (h + 1)] = got.reshape(16, 16, 128)

    copies[3].wait()

    def pack(i, _):
        low = parent_b[pl.ds(pl.multiple_of(i * 128, 128), 128), :].astype(F32)
        high = parent_b[pl.ds(pl.multiple_of(2048 + i * 128, 128), 128), :].astype(F32)
        both = jnp.concatenate([low, high], axis=1)
        parent_w[pl.ds(i * 16, 16)] = both.reshape(16, 8, 128)
        return 0

    lax.fori_loop(0, 16, pack, 0)
    lane_product(
        pfar, parent_w, lambda chunk, c: source[c % 4, chunk * 2 + c // 4], 2, 16, 4,
        lambda r, chunk: r * 16 + chunk,
    )
    lane = iota((256, 128), 1) // 2
    flat = pfar[...].reshape(256, 128)
    wide[0:16] = jnp.take_along_axis(flat, lane, axis=1).reshape(16, 16, 128)
    wide[16:32] = jnp.take_along_axis(flat, lane + 64, axis=1).reshape(16, 16, 128)

    first = place * 128 - 128
    rows = jnp.concatenate([before[0:512], own[0:512], after[0:512]], axis=1)
    for k in range(4):
        index = jnp.broadcast_to(leaf_lists[k : k + 1, :] - first, (384, 128))
        source[k] = dot(rows, picked(iota((384, 128), 0) == index)).reshape(32, 16, 128)
    copies[4].wait()
    widen(leaf_b, coupling_w)
    lane_product(
        far, coupling_w, lambda chunk, c: source[c % 4, chunk * 2 + c // 4], 4, 16, 4,
        lambda r, chunk: r * 16 + chunk,
    )
    copies[5].wait()
    widen(transfer, transfer_w)
    lane_product(
        far, transfer_w, lambda chunk, c: wide[chunk * 8 + c], 4, 4, 4,
        lambda a, chunk: a * 4 + chunk, start=far,
    )
    total = far[...].reshape(512, 128).astype(BF16)
    rows = jnp.concatenate([test[...].astype(F32), jnp.zeros((16, 128 - 32), F32)], axis=1)
    for h in range(2):
        payload[264 * h : 264 * h + 256, :] = total[256 * h : 256 * (h + 1)]
        payload[264 * h + 256 : 264 * h + 264, :] = rows[8 * h : 8 * (h + 1)].astype(BF16)
    for copy in fetched([(payload, out.at[i]) for i in range(out.shape[0])], sent):
        copy.wait()


def product_kernel(total_at, basis_at, out, total, basis, basis_w, total_w, grid, turned, sem):
    copies = fetched([(total_at.at[0], total), (basis_at, basis)], sem)
    for copy in copies:
        copy.wait()
    widen(basis, basis_w)
    for h in range(2):
        rows = total[264 * h : 264 * h + 256, :].astype(F32)
        total_w[16 * h : 16 * (h + 1)] = rows.reshape(16, 16, 128)

    def outer(blk, _):
        acc = weighted(
            8, 32, 16,
            lambda i, group, u: basis_w[(group * 16 + u) * 8 + blk, i : i + 1, :],
            lambda group, u: total_w[group * 16 + u],
            [jnp.zeros((16, 128), F32)] * 8,
        )
        for i in range(8):
            grid[blk * 8 + i] = acc[i]
        return 0

    lax.fori_loop(0, 8, outer, 0)
    even = picked(iota((64, 128), 1) == 2 * iota((64, 128), 0))
    odd = picked(iota((64, 128), 1) == 2 * iota((64, 128), 0) + 1)
    none = jnp.zeros((64, 128), BF16)
    for v in range(16):
        mine = grid[:, v, :].astype(BF16)
        turned[:, v, :] = dot(even, jnp.concatenate([mine, none], axis=0), ((1,), (1,))) + dot(
            odd, jnp.concatenate([none, mine], axis=0), ((1,), (1,))
        )
    for j in range(64):
        out[:, 128 * j : 128 * (j + 1)] = turned[j].astype(BF16)


def basis_kernel(
    mine_at, theirs_at, basis_at, new_at, fresh_at,
    totals, basis, basis_w, compressed, sketch, scale_w, gram, new_basis, fresh, sem, sent,
):
    groups = totals.shape[1]
    core = lax.rem(lax.axis_index("vector"), 2)
    copies = fetched(
        [(basis_at, basis), (mine_at, totals.at[core]), (theirs_at, totals.at[1 - core])], sem
    )
    copies[0].wait()
    widen(basis, basis_w)
    for copy in copies[1:]:
        copy.wait()
    pairs = [(g, h) for g in range(groups) for h in range(2)]
    tests = jnp.concatenate([totals[h, g, 256:264, :].astype(F32) for g, h in pairs], axis=0)
    across = tests.T[0:32].astype(BF16)
    for a in range(32):
        at = 16 * (a % 16)
        rows = jnp.concatenate([totals[a // 16, g, at : at + 16, :] for g in range(groups)], axis=0)
        compressed[a] = dot(across, rows)

    scale_w[...] = jnp.zeros((32, 128), F32)

    def outer(blk, _):
        acc = weighted(
            8, 32, 16,
            lambda i, group, u: basis_w[(group * 16 + u) * 8 + blk, i : i + 1, :],
            lambda group, u: compressed[group * 16 + u],
            [jnp.zeros((32, 128), F32)] * 8,
        )
        square = scale_w[...]
        for i in range(8):
            sketch[blk * 8 + i] = acc[i]
            square = square + acc[i] * acc[i]
        scale_w[...] = square
        return 0

    lax.fori_loop(0, 8, outer, 0)
    scale_w[...] = lax.rsqrt(scale_w[...] / 64 + 1e-06)

    def scaled(group, _):
        scale = scale_w[...]
        for u in range(8):
            new_basis[group * 8 + u] = sketch[group * 8 + u] * scale
        return 0

    lax.fori_loop(0, 8, scaled, 0)
    first = fetched([(new_basis, new_at)], sent)

    for tile in range(4):
        low = 8 * tile
        acc = weighted(
            8, 64, 16,
            lambda i, group, u: sketch[group * 16 + u, low + i : low + i + 1, :],
            lambda group, u: sketch[group * 16 + u, low:32, :],
            [jnp.zeros((32 - low, 128), F32)] * 8,
        )
        for i in range(8):
            gram[(low + i) * 32 + low : (low + i) * 32 + 32, :] = acc[i]
    for a in range(32):
        row = scale_w[a : a + 1, :] * (1.0 / 64)
        low = a // 8 * 8
        fresh[a, low:32, :] = gram[a * 32 + low : a * 32 + 32, :] * row
        for b in range(0, low, 8):
            fresh[a, b : b + 8, :] = gram[pl.ds(b * 32 + a, 8, stride=32), :] * row
    second = pltpu.make_async_copy(fresh, fresh_at, sent.at[1])
    second.start()
    first[0].wait()
    second.wait()


def shards(
    samples, leaf_basis_matrix, transfer, leaf_lists, leaf_coupling, parent_lists,
    parent_coupling, test_matrix,
):
    basis = leaf_basis_matrix.reshape(2048, 128)
    moves = transfer.reshape(1024, 128)
    near = leaf_coupling.reshape(4096, 128)
    above = parent_coupling.reshape(4096, 64)
    vmem = pl.BlockSpec(memory_space=pltpu.VMEM)
    anywhere = pl.BlockSpec(memory_space=pl.ANY)
    stored = pl.BlockSpec(memory_space=pltpu.HBM)

    coeff = pl.pallas_call(
        coeff_kernel,
        out_shape=jax.ShapeDtypeStruct((768, 128), BF16),
        in_specs=[stored] * 3,
        out_specs=vmem,
        scratch_shapes=[
            pltpu.VMEM((16, 8192), BF16),
            pltpu.VMEM((2048, 128), BF16),
            pltpu.VMEM((1024, 128), BF16),
            pltpu.VMEM((256, 8, 128), F32),
            pltpu.VMEM((128, 8, 128), F32),
            pltpu.VMEM((1024, 128), F32),
            pltpu.VMEM((64, 16, 128), F32),
            pltpu.VMEM((32, 16, 128), F32),
            pltpu.VMEM((32, 16, 128), F32),
            pltpu.SemaphoreType.DMA((3,)),
        ],
        compiler_params=pltpu.CompilerParams(vmem_limit_bytes=24 << 20),
        name="coeff",
    )(samples, basis, moves)

    peers = lax.axis_size("cluster") * lax.axis_size("replica")
    up = [(i, i + 1) for i in range(peers - 1)]
    before = lax.ppermute(coeff, HOPS, up)
    after = lax.ppermute(coeff, HOPS, [(b, a) for a, b in up])

    groups = lax.axis_size("vector")
    half = groups // 2
    total = pl.pallas_call(
        far_kernel,
        out_shape=jax.ShapeDtypeStruct((half, 528, 128), BF16),
        in_specs=[anywhere] * 3 + [stored] * 3 + [vmem] * 3,
        out_specs=anywhere,
        scratch_shapes=[
            pltpu.VMEM((768, 128), BF16),
            pltpu.VMEM((768, 128), BF16),
            pltpu.VMEM((768, 128), BF16),
            pltpu.VMEM((1024, 128), BF16),
            pltpu.VMEM((4096, 128), BF16),
            pltpu.VMEM((4096, 64), BF16),
            pltpu.VMEM((512, 8, 128), F32),
            pltpu.VMEM((256, 8, 128), F32),
            pltpu.VMEM((128, 8, 128), F32),
            pltpu.VMEM((4, 32, 16, 128), F32),
            pltpu.VMEM((32, 16, 128), F32),
            pltpu.VMEM((16, 16, 128), F32),
            pltpu.VMEM((32, 16, 128), F32),
            pltpu.VMEM((528, 128), BF16),
            pltpu.SemaphoreType.DMA((6,)),
            pltpu.SemaphoreType.DMA((half,)),
        ],
        compiler_params=pltpu.CompilerParams(vmem_limit_bytes=24 << 20),
        name="far",
    )(coeff, before, after, moves, near, above, leaf_lists, parent_lists, test_matrix)

    mine = lax.all_to_all(total.reshape(groups, 264, 128), "vector", 0, 0, tiled=True)
    product = pl.pallas_call(
        product_kernel,
        out_shape=jax.ShapeDtypeStruct((16, 8192), BF16),
        in_specs=[anywhere] * 2,
        out_specs=vmem,
        scratch_shapes=[
            pltpu.VMEM((528, 128), BF16),
            pltpu.VMEM((2048, 128), BF16),
            pltpu.VMEM((256, 8, 128), F32),
            pltpu.VMEM((32, 16, 128), F32),
            pltpu.VMEM((64, 16, 128), F32),
            pltpu.VMEM((64, 16, 128), F32),
            pltpu.SemaphoreType.DMA((2,)),
        ],
        cost_estimate=pl.CostEstimate(flops=10**7, bytes_accessed=10**6, transcendentals=0),
        compiler_params=pltpu.CompilerParams(vmem_limit_bytes=24 << 20),
        name="product",
    )(total, basis)

    mine, product = lax.optimization_barrier((mine, product))
    theirs = lax.ppermute(mine, "vector", [(i, i ^ 1) for i in range(groups)])

    new_basis, fresh = pl.pallas_call(
        basis_kernel,
        out_shape=(
            jax.ShapeDtypeStruct((64, 32, 128), F32),
            jax.ShapeDtypeStruct((32, 32, 128), F32),
        ),
        in_specs=[anywhere] * 3,
        out_specs=(anywhere, anywhere),
        scratch_shapes=[
            pltpu.VMEM((2, groups, 264, 128), BF16),
            pltpu.VMEM((2048, 128), BF16),
            pltpu.VMEM((256, 8, 128), F32),
            pltpu.VMEM((32, 32, 128), F32),
            pltpu.VMEM((64, 32, 128), F32),
            pltpu.VMEM((32, 128), F32),
            pltpu.VMEM((1024, 128), F32),
            pltpu.VMEM((64, 32, 128), F32),
            pltpu.VMEM((32, 32, 128), F32),
            pltpu.SemaphoreType.DMA((3,)),
            pltpu.SemaphoreType.DMA((2,)),
        ],
        compiler_params=pltpu.CompilerParams(vmem_limit_bytes=24 << 20),
        name="basis",
    )(mine, theirs, basis)
    return product, new_basis, fresh


def solution(mesh):
    placed = (
        P("vector", HOPS),
        P(None, None, HOPS),
        P(None, None, HOPS),
        P(None, HOPS),
        P(None, None, None, HOPS),
        P(None, HOPS),
        P(None, None, None, HOPS),
        P("vector", None),
    )
    return jax.shard_map(
        shards,
        mesh=mesh,
        in_specs=placed,
        out_specs=(P("vector", HOPS), P(None, None, HOPS), P(None, None, HOPS)),
        check_vma=False,
    )
```

```python
import jax
import jax.numpy as jnp
from jax import lax
from jax.experimental import pallas as pl
from jax.experimental.pallas import tpu as pltpu
from jax.sharding import PartitionSpec as P

F32, BF16 = jnp.float32, jnp.bfloat16
HOPS = ("cluster", "replica")


def iota(shape, dim):
    return lax.broadcasted_iota(jnp.int32, shape, dim)


def picked(mask):
    return jnp.where(mask, 1.0, 0.0).astype(BF16)


def dot(a, b, contract=((1,), (0,))):
    return lax.dot_general(a, b, (contract, ((), ())), preferred_element_type=F32)


def widen(src, dst, step=128):
    tiles = step // 8

    def body(i, _):
        rows = src[pl.ds(pl.multiple_of(i * step, step), step), :].astype(F32)
        dst[pl.ds(i * tiles, tiles)] = rows.reshape(tiles, 8, rows.shape[-1])
        return 0

    lax.fori_loop(0, src.shape[0] // step, body, 0)


def weighted(block, steps, unroll, weight, term, init):
    def body(group, acc):
        acc = list(acc)
        for u in range(unroll):
            src = term(group, u)
            for i in range(block):
                acc[i] = acc[i] + weight(i, group, u) * src
        return tuple(acc)

    return lax.fori_loop(0, steps // unroll, body, tuple(init))


def lane_product(out, left, right_of, blocks, chunks, per, tile_of, start=None, block=8):
    rows, wide = out.shape[1:]

    def outer(blk, _):
        first = [blk * block + i for i in range(block)]
        init = [jnp.zeros((rows, wide), F32) if start is None else start[o] for o in first]

        def weight(i, group, u):
            c = u % 8
            return left[tile_of(first[i], group * per + u // 8), c : c + 1, :]

        acc = weighted(
            block, chunks * 8, per * 8, weight,
            lambda group, u: right_of(group * per + u // 8, u % 8), init,
        )
        for i, o in enumerate(first):
            out[o] = acc[i]
        return 0

    lax.fori_loop(0, blocks, outer, 0)


def swaps(firsts):
    return [pair for i in firsts for pair in ((i, i + 1), (i + 1, i))]


def fetched(pairs, sem):
    copies = [pltpu.make_async_copy(a, b, sem.at[i]) for i, (a, b) in enumerate(pairs)]
    for copy in copies:
        copy.start()
    return copies


def coeff_kernel(
    samples_at, basis_at, transfer_at, out,
    samples, basis, transfer, basis_w, transfer_w, xj, points, leaf, parent, sem,
):
    copies = fetched(
        [(samples_at, samples), (basis_at, basis), (transfer_at, transfer)], sem
    )
    vecs = samples.shape[0]
    even = picked(iota((64, 128), 1) == 2 * iota((64, 128), 0))
    odd = picked(iota((64, 128), 1) == 2 * iota((64, 128), 0) + 1)
    copies[0].wait()
    for j in range(64):
        xj[pl.ds(j * vecs, vecs), :] = samples[:, 128 * j : 128 * (j + 1)].astype(F32)
    for v in range(vecs):
        turned = xj[pl.ds(v, 64, stride=vecs), :].T
        both = dot(turned[:64].astype(BF16), even) + dot(turned[64:].astype(BF16), odd)
        points[:, v, :] = both
    copies[1].wait()
    widen(basis, basis_w)
    lane_product(
        leaf, basis_w, lambda chunk, c: points[chunk * 8 + c], 4, 8, 4,
        lambda r, chunk: r * 8 + chunk,
    )
    rounded = leaf[...].astype(BF16)
    out[0:512, :] = rounded.reshape(512, 128)
    leaf[...] = rounded.astype(F32)
    copies[2].wait()
    widen(transfer, transfer_w)

    def outer(blk, _):
        acc = weighted(
            8, 32, 16,
            lambda i, group, u: transfer_w[(group * 16 + u) * 4 + blk, i : i + 1, :],
            lambda group, u: leaf[group * 16 + u],
            [jnp.zeros((vecs, 128), F32)] * 8,
        )
        for i in range(8):
            parent[blk * 8 + i] = acc[i] + pltpu.roll(acc[i], 127, 1)
        return 0

    lax.fori_loop(0, 4, outer, 0)
    low = picked(iota((128, 128), 0) == 2 * iota((128, 128), 1))
    high = picked(iota((128, 128), 0) == 2 * iota((128, 128), 1) - 128)
    sums = parent[...].reshape(512, 128).astype(BF16)
    out[512:768, :] = (dot(sums[0:256], low) + dot(sums[256:512], high)).astype(BF16)


def far_kernel(
    own_at, inner_at, outer_at, transfer_at, leaf_at, parent_at, leaf_lists, parent_lists, test,
    out, own, sides, transfer, leaf_b, parent_b,
    coupling_w, parent_w, transfer_w, source, far, pfar, wide, payload, sem, sent,
):
    place = lax.axis_index("cluster") * lax.axis_size("replica") + lax.axis_index("replica")
    odd = lax.rem(place, 2)
    before, after = sides.at[0], sides.at[1]
    copies = fetched(
        [
            (own_at, own), (inner_at, sides.at[1 - odd]), (outer_at, sides.at[odd]),
            (parent_at, parent_b), (leaf_at, leaf_b), (transfer_at, transfer),
        ],
        sem,
    )

    first = place * 64 - 64
    twice = picked(iota((64, 128), 0) == iota((64, 128), 1) % 64)
    none = jnp.zeros((64, 128), BF16)
    for copy in copies[:3]:
        copy.wait()
    packed = jnp.concatenate([before[512:768], own[512:768], after[512:768]], axis=1)
    for k in range(4):
        index = jnp.broadcast_to(parent_lists[k : k + 1, :] - first, (64, 64))
        hits = [
            dot(picked(iota((64, 64), 0) + 64 * m == index), twice).astype(BF16) for m in range(3)
        ]
        for h in range(2):
            parts = [part for hit in hits for part in ((hit, none) if h == 0 else (none, hit))]
            got = dot(packed, jnp.concatenate(parts, axis=0))
            source[k, 16 * h : 16 * (h + 1)] = got.reshape(16, 16, 128)

    copies[3].wait()

    def pack(i, _):
        low = parent_b[pl.ds(pl.multiple_of(i * 128, 128), 128), :].astype(F32)
        high = parent_b[pl.ds(pl.multiple_of(2048 + i * 128, 128), 128), :].astype(F32)
        both = jnp.concatenate([low, high], axis=1)
        parent_w[pl.ds(i * 16, 16)] = both.reshape(16, 8, 128)
        return 0

    lax.fori_loop(0, 16, pack, 0)
    lane_product(
        pfar, parent_w, lambda chunk, c: source[c % 4, chunk * 2 + c // 4], 2, 16, 4,
        lambda r, chunk: r * 16 + chunk,
    )
    lane = iota((256, 128), 1) // 2
    flat = pfar[...].reshape(256, 128)
    wide[0:16] = jnp.take_along_axis(flat, lane, axis=1).reshape(16, 16, 128)
    wide[16:32] = jnp.take_along_axis(flat, lane + 64, axis=1).reshape(16, 16, 128)

    first = place * 128 - 128
    rows = jnp.concatenate([before[0:512], own[0:512], after[0:512]], axis=1)
    for k in range(4):
        index = jnp.broadcast_to(leaf_lists[k : k + 1, :] - first, (384, 128))
        source[k] = dot(rows, picked(iota((384, 128), 0) == index)).reshape(32, 16, 128)
    copies[4].wait()
    widen(leaf_b, coupling_w)
    lane_product(
        far, coupling_w, lambda chunk, c: source[c % 4, chunk * 2 + c // 4], 4, 16, 4,
        lambda r, chunk: r * 16 + chunk,
    )
    copies[5].wait()
    widen(transfer, transfer_w)
    lane_product(
        far, transfer_w, lambda chunk, c: wide[chunk * 8 + c], 4, 4, 4,
        lambda a, chunk: a * 4 + chunk, start=far,
    )
    total = far[...].reshape(512, 128).astype(BF16)
    rows = jnp.concatenate([test[...].astype(F32), jnp.zeros((16, 128 - 32), F32)], axis=1)
    for h in range(2):
        payload[264 * h : 264 * h + 256, :] = total[256 * h : 256 * (h + 1)]
        payload[264 * h + 256 : 264 * h + 264, :] = rows[8 * h : 8 * (h + 1)].astype(BF16)
    for copy in fetched([(payload, out.at[i]) for i in range(out.shape[0])], sent):
        copy.wait()


def product_kernel(total_at, basis_at, out, total, basis, basis_w, total_w, grid, turned, sem):
    copies = fetched([(total_at.at[0], total), (basis_at, basis)], sem)
    for copy in copies:
        copy.wait()
    widen(basis, basis_w)
    for h in range(2):
        rows = total[264 * h : 264 * h + 256, :].astype(F32)
        total_w[16 * h : 16 * (h + 1)] = rows.reshape(16, 16, 128)

    def outer(blk, _):
        acc = weighted(
            8, 32, 16,
            lambda i, group, u: basis_w[(group * 16 + u) * 8 + blk, i : i + 1, :],
            lambda group, u: total_w[group * 16 + u],
            [jnp.zeros((16, 128), F32)] * 8,
        )
        for i in range(8):
            grid[blk * 8 + i] = acc[i]
        return 0

    lax.fori_loop(0, 8, outer, 0)
    even = picked(iota((64, 128), 1) == 2 * iota((64, 128), 0))
    odd = picked(iota((64, 128), 1) == 2 * iota((64, 128), 0) + 1)
    none = jnp.zeros((64, 128), BF16)
    for v in range(16):
        mine = grid[:, v, :].astype(BF16)
        turned[:, v, :] = dot(even, jnp.concatenate([mine, none], axis=0), ((1,), (1,))) + dot(
            odd, jnp.concatenate([none, mine], axis=0), ((1,), (1,))
        )
    for j in range(64):
        out[:, 128 * j : 128 * (j + 1)] = turned[j].astype(BF16)


def basis_kernel(
    mine_at, theirs_at, basis_at, new_at, fresh_at,
    totals, basis, basis_w, compressed, sketch, scale_w, gram, new_basis, fresh, sem, sent,
):
    groups = totals.shape[1]
    core = lax.rem(lax.axis_index("vector"), 2)
    copies = fetched(
        [(basis_at, basis), (mine_at, totals.at[core]), (theirs_at, totals.at[1 - core])], sem
    )
    copies[0].wait()
    widen(basis, basis_w)
    for copy in copies[1:]:
        copy.wait()
    pairs = [(g, h) for g in range(groups) for h in range(2)]
    tests = jnp.concatenate([totals[h, g, 256:264, :].astype(F32) for g, h in pairs], axis=0)
    across = tests.T[0:32].astype(BF16)
    for a in range(32):
        at = 16 * (a % 16)
        rows = jnp.concatenate([totals[a // 16, g, at : at + 16, :] for g in range(groups)], axis=0)
        compressed[a] = dot(across, rows)

    scale_w[...] = jnp.zeros((32, 128), F32)

    def outer(blk, _):
        acc = weighted(
            8, 32, 16,
            lambda i, group, u: basis_w[(group * 16 + u) * 8 + blk, i : i + 1, :],
            lambda group, u: compressed[group * 16 + u],
            [jnp.zeros((32, 128), F32)] * 8,
        )
        square = scale_w[...]
        for i in range(8):
            sketch[blk * 8 + i] = acc[i]
            square = square + acc[i] * acc[i]
        scale_w[...] = square
        return 0

    lax.fori_loop(0, 8, outer, 0)
    scale_w[...] = lax.rsqrt(scale_w[...] / 64 + 1e-06)

    def scaled(group, _):
        scale = scale_w[...]
        for u in range(8):
            new_basis[group * 8 + u] = sketch[group * 8 + u] * scale
        return 0

    lax.fori_loop(0, 8, scaled, 0)
    first = fetched([(new_basis, new_at)], sent)

    for tile in range(4):
        low = 8 * tile
        acc = weighted(
            8, 64, 16,
            lambda i, group, u: sketch[group * 16 + u, low + i : low + i + 1, :],
            lambda group, u: sketch[group * 16 + u, low:32, :],
            [jnp.zeros((32 - low, 128), F32)] * 8,
        )
        for i in range(8):
            gram[(low + i) * 32 + low : (low + i) * 32 + 32, :] = acc[i]
    for a in range(32):
        row = scale_w[a : a + 1, :] * (1.0 / 64)
        low = a // 8 * 8
        fresh[a, low:32, :] = gram[a * 32 + low : a * 32 + 32, :] * row
        for b in range(0, low, 8):
            fresh[a, b : b + 8, :] = gram[pl.ds(b * 32 + a, 8, stride=32), :] * row
    second = pltpu.make_async_copy(fresh, fresh_at, sent.at[1])
    second.start()
    first[0].wait()
    second.wait()


def shards(
    samples, leaf_basis_matrix, transfer, leaf_lists, leaf_coupling, parent_lists,
    parent_coupling, test_matrix,
):
    basis = leaf_basis_matrix.reshape(2048, 128)
    moves = transfer.reshape(1024, 128)
    near = leaf_coupling.reshape(4096, 128)
    above = parent_coupling.reshape(4096, 64)
    vmem = pl.BlockSpec(memory_space=pltpu.VMEM)
    anywhere = pl.BlockSpec(memory_space=pl.ANY)

    coeff = pl.pallas_call(
        coeff_kernel,
        out_shape=jax.ShapeDtypeStruct((768, 128), BF16),
        in_specs=[anywhere] * 3,
        out_specs=vmem,
        scratch_shapes=[
            pltpu.VMEM((16, 8192), BF16),
            pltpu.VMEM((2048, 128), BF16),
            pltpu.VMEM((1024, 128), BF16),
            pltpu.VMEM((256, 8, 128), F32),
            pltpu.VMEM((128, 8, 128), F32),
            pltpu.VMEM((1024, 128), F32),
            pltpu.VMEM((64, 16, 128), F32),
            pltpu.VMEM((32, 16, 128), F32),
            pltpu.VMEM((32, 16, 128), F32),
            pltpu.SemaphoreType.DMA((3,)),
        ],
        compiler_params=pltpu.CompilerParams(vmem_limit_bytes=62 << 20),
        name="coeff",
    )(samples, basis, moves)

    peers = lax.axis_size("cluster") * lax.axis_size("replica")
    outer = lax.ppermute(coeff, HOPS, swaps(range(1, peers - 1, 2)))
    inner = lax.ppermute(coeff, HOPS, swaps(range(0, peers - 1, 2)))

    groups = lax.axis_size("vector")
    half = groups // 2
    total = pl.pallas_call(
        far_kernel,
        out_shape=jax.ShapeDtypeStruct((half, 528, 128), BF16),
        in_specs=[anywhere] * 3 + [anywhere] * 3 + [vmem] * 3,
        out_specs=anywhere,
        scratch_shapes=[
            pltpu.VMEM((768, 128), BF16),
            pltpu.VMEM((2, 768, 128), BF16),
            pltpu.VMEM((1024, 128), BF16),
            pltpu.VMEM((4096, 128), BF16),
            pltpu.VMEM((4096, 64), BF16),
            pltpu.VMEM((512, 8, 128), F32),
            pltpu.VMEM((256, 8, 128), F32),
            pltpu.VMEM((128, 8, 128), F32),
            pltpu.VMEM((4, 32, 16, 128), F32),
            pltpu.VMEM((32, 16, 128), F32),
            pltpu.VMEM((16, 16, 128), F32),
            pltpu.VMEM((32, 16, 128), F32),
            pltpu.VMEM((528, 128), BF16),
            pltpu.SemaphoreType.DMA((6,)),
            pltpu.SemaphoreType.DMA((half,)),
        ],
        compiler_params=pltpu.CompilerParams(vmem_limit_bytes=62 << 20),
        name="far",
    )(coeff, inner, outer, moves, near, above, leaf_lists, parent_lists, test_matrix)

    mine = lax.all_to_all(total.reshape(groups, 264, 128), "vector", 0, 0, tiled=True)
    product = pl.pallas_call(
        product_kernel,
        out_shape=jax.ShapeDtypeStruct((16, 8192), BF16),
        in_specs=[anywhere] * 2,
        out_specs=vmem,
        scratch_shapes=[
            pltpu.VMEM((528, 128), BF16),
            pltpu.VMEM((2048, 128), BF16),
            pltpu.VMEM((256, 8, 128), F32),
            pltpu.VMEM((32, 16, 128), F32),
            pltpu.VMEM((64, 16, 128), F32),
            pltpu.VMEM((64, 16, 128), F32),
            pltpu.SemaphoreType.DMA((2,)),
        ],
        cost_estimate=pl.CostEstimate(flops=10**7, bytes_accessed=10**6, transcendentals=0),
        compiler_params=pltpu.CompilerParams(vmem_limit_bytes=24 << 20),
        name="product",
    )(total, basis)

    mine, product = lax.optimization_barrier((mine, product))
    theirs = lax.ppermute(mine, "vector", [(i, i ^ 1) for i in range(groups)])

    new_basis, fresh = pl.pallas_call(
        basis_kernel,
        out_shape=(
            jax.ShapeDtypeStruct((64, 32, 128), F32),
            jax.ShapeDtypeStruct((32, 32, 128), F32),
        ),
        in_specs=[anywhere] * 3,
        out_specs=(anywhere, anywhere),
        scratch_shapes=[
            pltpu.VMEM((2, groups, 264, 128), BF16),
            pltpu.VMEM((2048, 128), BF16),
            pltpu.VMEM((256, 8, 128), F32),
            pltpu.VMEM((32, 32, 128), F32),
            pltpu.VMEM((64, 32, 128), F32),
            pltpu.VMEM((32, 128), F32),
            pltpu.VMEM((1024, 128), F32),
            pltpu.VMEM((64, 32, 128), F32),
            pltpu.VMEM((32, 32, 128), F32),
            pltpu.SemaphoreType.DMA((3,)),
            pltpu.SemaphoreType.DMA((2,)),
        ],
        compiler_params=pltpu.CompilerParams(vmem_limit_bytes=24 << 20),
        name="basis",
    )(mine, theirs, basis)
    return product, new_basis, fresh


def solution(mesh):
    placed = (
        P("vector", HOPS),
        P(None, None, HOPS),
        P(None, None, HOPS),
        P(None, HOPS),
        P(None, None, None, HOPS),
        P(None, HOPS),
        P(None, None, None, HOPS),
        P("vector", None),
    )
    return jax.shard_map(
        shards,
        mesh=mesh,
        in_specs=placed,
        out_specs=(P("vector", HOPS), P(None, None, HOPS), P(None, None, HOPS)),
        check_vma=False,
    )
```

```python
import jax
import jax.numpy as jnp
from jax import lax
from jax.experimental import pallas as pl
from jax.experimental.pallas import tpu as pltpu
from jax.sharding import PartitionSpec as P

F32, BF16 = jnp.float32, jnp.bfloat16
HOPS = ("cluster", "replica")


def iota(shape, dim):
    return lax.broadcasted_iota(jnp.int32, shape, dim)


def picked(mask):
    return jnp.where(mask, 1.0, 0.0).astype(BF16)


def dot(a, b, contract=((1,), (0,))):
    return lax.dot_general(a, b, (contract, ((), ())), preferred_element_type=F32)


def widen(src, dst, step=128):
    tiles = step // 8

    def body(i, _):
        rows = src[pl.ds(pl.multiple_of(i * step, step), step), :].astype(F32)
        dst[pl.ds(i * tiles, tiles)] = rows.reshape(tiles, 8, rows.shape[-1])
        return 0

    lax.fori_loop(0, src.shape[0] // step, body, 0)


def weighted(block, steps, unroll, weight, term, init):
    def body(group, acc):
        acc = list(acc)
        for u in range(unroll):
            src = term(group, u)
            for i in range(block):
                acc[i] = acc[i] + weight(i, group, u) * src
        return tuple(acc)

    return lax.fori_loop(0, steps // unroll, body, tuple(init))


def lane_product(out, left, right_of, blocks, chunks, per, tile_of, start=None, block=8, at=0):
    rows, wide = out.shape[1:]

    def outer(blk, _):
        first = [at + blk * block + i for i in range(block)]
        init = [jnp.zeros((rows, wide), F32) if start is None else start[o] for o in first]

        def weight(i, group, u):
            c = u % 8
            return left[tile_of(first[i], group * per + u // 8), c : c + 1, :]

        acc = weighted(
            block, chunks * 8, per * 8, weight,
            lambda group, u: right_of(group * per + u // 8, u % 8), init,
        )
        for i, o in enumerate(first):
            out[o] = acc[i]
        return 0

    lax.fori_loop(0, blocks, outer, 0)


def swaps(firsts):
    return [pair for i in firsts for pair in ((i, i + 1), (i + 1, i))]


def fetched(pairs, sem):
    copies = [pltpu.make_async_copy(a, b, sem.at[i]) for i, (a, b) in enumerate(pairs)]
    for copy in copies:
        copy.start()
    return copies


def coeff_kernel(
    samples_at, basis_at, transfer_at, out,
    samples, basis, transfer, basis_w, transfer_w, xj, points, leaf, parent, sem,
):
    copies = fetched(
        [(samples_at, samples), (basis_at, basis), (transfer_at, transfer)], sem
    )
    vecs = samples.shape[0]
    row, col = iota((256, 256), 0), iota((256, 256), 1)
    spread = picked(
        (row // 64 % 2 == col // 128) & (col % 128 == 2 * (row % 64) + row // 128)
    )
    copies[0].wait()
    for j in range(64):
        xj[pl.ds(j * vecs, vecs), :] = samples[:, 128 * j : 128 * (j + 1)].astype(F32)
    for v in range(0, vecs, 2):
        pair = [xj[pl.ds(v + i, 64, stride=vecs), :] for i in range(2)]
        turned = jnp.concatenate(pair, axis=0).T
        both = dot(
            jnp.concatenate([turned[:64], turned[64:]], axis=1).astype(BF16), spread
        )
        for i in range(2):
            points[pl.ds(v + i, 64, stride=vecs), :] = both[:, 128 * i : 128 * (i + 1)]
    copies[1].wait()
    widen(basis, basis_w)
    lane_product(
        leaf, basis_w,
        lambda chunk, c: points[pl.ds(pl.multiple_of((chunk * 8 + c) * vecs, 16), vecs), :], 4, 8, 4,
        lambda r, chunk: r * 8 + chunk,
    )
    rounded = leaf[...].astype(BF16)
    out[0:512, :] = rounded.reshape(512, 128)
    leaf[...] = rounded.astype(F32)
    copies[2].wait()
    widen(transfer, transfer_w)

    def outer(blk, _):
        acc = weighted(
            8, 32, 16,
            lambda i, group, u: transfer_w[(group * 16 + u) * 4 + blk, i : i + 1, :],
            lambda group, u: leaf[group * 16 + u],
            [jnp.zeros((vecs, 128), F32)] * 8,
        )
        for i in range(8):
            parent[blk * 8 + i] = acc[i] + pltpu.roll(acc[i], 127, 1)
        return 0

    lax.fori_loop(0, 4, outer, 0)
    low = picked(iota((128, 128), 0) == 2 * iota((128, 128), 1))
    high = picked(iota((128, 128), 0) == 2 * iota((128, 128), 1) - 128)
    sums = parent[...].reshape(512, 128).astype(BF16)
    out[512:768, :] = (dot(sums[0:256], low) + dot(sums[256:512], high)).astype(BF16)


def far_kernel(
    own_at, inner_at, outer_at, transfer_at, leaf_at, parent_at, leaf_lists, parent_lists, test,
    out, own, sides, transfer, leaf_b, parent_b,
    coupling_w, parent_w, transfer_w, source, far, pfar, wide, payload, sem, sent,
):
    place = lax.axis_index("cluster") * lax.axis_size("replica") + lax.axis_index("replica")
    odd = lax.rem(place, 2)
    before, after = sides.at[0], sides.at[1]
    copies = fetched(
        [
            (own_at, own), (inner_at, sides.at[1 - odd]), (outer_at, sides.at[odd]),
            (parent_at, parent_b), (leaf_at, leaf_b), (transfer_at, transfer),
        ],
        sem,
    )

    first = place * 64 - 64
    none = jnp.zeros((64, 128), BF16)
    lists = jnp.concatenate([parent_lists[...], parent_lists[...]], axis=1) - first
    for copy in copies[:3]:
        copy.wait()
    packed = jnp.concatenate([before[512:768], own[512:768], after[512:768]], axis=1)
    for k in range(4):
        index = jnp.broadcast_to(lists[k : k + 1, :], (64, 128))
        parts = []
        for m in range(3):
            hit = picked(iota((64, 128), 0) + 64 * m == index)
            parts += [jnp.concatenate(two, axis=1) for two in ((hit, none), (none, hit))]
        got = dot(packed, jnp.concatenate(parts, axis=0))
        for h in range(2):
            part = got[:, 128 * h : 128 * (h + 1)]
            source[k, 16 * h : 16 * (h + 1)] = part.reshape(16, 16, 128)

    copies[3].wait()

    def pack(i, _):
        low = parent_b[pl.ds(pl.multiple_of(i * 128, 128), 128), :].astype(F32)
        high = parent_b[pl.ds(pl.multiple_of(2048 + i * 128, 128), 128), :].astype(F32)
        both = jnp.concatenate([low, high], axis=1)
        parent_w[pl.ds(i * 16, 16)] = both.reshape(16, 8, 128)
        return 0

    lax.fori_loop(0, 16, pack, 0)
    lane_product(
        pfar, parent_w, lambda chunk, c: source[c % 4, chunk * 2 + c // 4], 2, 16, 4,
        lambda r, chunk: r * 16 + chunk,
    )
    lane = iota((256, 128), 1) // 2
    flat = pfar[...].reshape(256, 128)
    wide[0:16] = jnp.take_along_axis(flat, lane, axis=1).reshape(16, 16, 128)
    wide[16:32] = jnp.take_along_axis(flat, lane + 64, axis=1).reshape(16, 16, 128)

    first = place * 128 - 128
    rows = jnp.concatenate([before[0:512], own[0:512], after[0:512]], axis=1)
    for k in range(0, 4, 2):
        hits = [
            picked(
                iota((384, 128), 0)
                == jnp.broadcast_to(leaf_lists[k + i : k + i + 1, :] - first, (384, 128))
            )
            for i in range(2)
        ]
        got = dot(rows, jnp.concatenate(hits, axis=1))
        for i in range(2):
            source[k + i] = got[:, 128 * i : 128 * (i + 1)].reshape(32, 16, 128)
    copies[4].wait()
    widen(leaf_b, coupling_w)
    lane_product(
        far, coupling_w, lambda chunk, c: source[c % 4, chunk * 2 + c // 4], 4, 16, 4,
        lambda r, chunk: r * 16 + chunk,
    )
    copies[5].wait()
    widen(transfer, transfer_w)
    rows = jnp.concatenate([test[...].astype(F32), jnp.zeros((16, 128 - 32), F32)], axis=1)
    copies = []
    for h in range(2):
        lane_product(
            far, transfer_w, lambda chunk, c: wide[chunk * 8 + c], 2, 4, 4,
            lambda a, chunk: a * 4 + chunk, start=far, at=16 * h,
        )
        payload[h, 0:256, :] = far[16 * h : 16 * (h + 1)].reshape(256, 128).astype(BF16)
        payload[h, 256:272, :] = rows.astype(BF16)
        for y in range(out.shape[0] // 2):
            copy = pltpu.make_async_copy(payload.at[h], out.at[2 * y + h], sent.at[2 * y + h])
            copy.start()
            copies.append(copy)
    for copy in copies:
        copy.wait()


def product_kernel(total_at, basis_at, out, total, basis, basis_w, total_w, grid, turned, sem):
    copies = fetched([(total_at.at[0:2], total), (basis_at, basis)], sem)
    for copy in copies:
        copy.wait()
    widen(basis, basis_w)
    for h in range(2):
        rows = total[h, 0:256, :].astype(F32)
        total_w[16 * h : 16 * (h + 1)] = rows.reshape(16, 16, 128)

    def outer(blk, _):
        acc = weighted(
            8, 32, 16,
            lambda i, group, u: basis_w[(group * 16 + u) * 8 + blk, i : i + 1, :],
            lambda group, u: total_w[group * 16 + u],
            [jnp.zeros((16, 128), F32)] * 8,
        )
        for i in range(8):
            grid[pl.ds(pl.multiple_of((blk * 8 + i) * 16, 16), 16), :] = acc[i]
        return 0

    lax.fori_loop(0, 8, outer, 0)
    even = picked(iota((64, 128), 1) == 2 * iota((64, 128), 0))
    odd = picked(iota((64, 128), 1) == 2 * iota((64, 128), 0) + 1)
    none = jnp.zeros((64, 128), BF16)
    for v in range(16):
        mine = grid[pl.ds(v, 64, stride=16), :].astype(BF16)
        turned[pl.ds(v, 64, stride=16), :] = dot(even, jnp.concatenate([mine, none], axis=0), ((1,), (1,))) + dot(
            odd, jnp.concatenate([none, mine], axis=0), ((1,), (1,))
        )
    for j in range(64):
        out[:, 128 * j : 128 * (j + 1)] = turned[16 * j : 16 * (j + 1), :].astype(BF16)


def compress(halves, compressed):
    groups = range(halves.shape[0])
    tests = jnp.concatenate([halves[g, 256:272, :] for g in groups], axis=0)
    across = tests.astype(F32).T[0:32].astype(BF16)
    for a in range(16):
        rows = jnp.concatenate([halves[g, 16 * a : 16 * (a + 1), :] for g in groups], axis=0)
        compressed[a] = dot(across, rows)


def part_kernel(mine_at, basis_at, out, halves, basis, basis_w, compressed, partial, sem, sent):
    core = lax.rem(lax.axis_index("vector"), 2)
    ranks = pl.ds(pl.multiple_of(core * 1024, 1024), 1024)
    copies = fetched([(basis_at.at[ranks], basis), (mine_at, halves)], sem)
    copies[0].wait()
    widen(basis, basis_w)
    copies[1].wait()
    compress(halves, compressed)

    def outer(blk, _):
        acc = weighted(
            8, 16, 16,
            lambda i, group, u: basis_w[u * 8 + blk, i : i + 1, :],
            lambda group, u: compressed[u],
            [jnp.zeros((32, 128), F32)] * 8,
        )
        for i in range(8):
            partial[blk * 8 + i] = acc[i]
        return 0

    lax.fori_loop(0, 8, outer, 0)
    for copy in fetched([(partial, out)], sent):
        copy.wait()


def basis_kernel(
    theirs_at, partial_at, basis_at, new_at, fresh_at,
    halves, basis, basis_w, compressed, sketch, scale_w, gram, new_basis, fresh, sem, sent,
):
    core = 1 - lax.rem(lax.axis_index("vector"), 2)
    ranks = pl.ds(pl.multiple_of(core * 1024, 1024), 1024)
    copies = fetched(
        [(basis_at.at[ranks], basis), (theirs_at, halves), (partial_at, sketch)], sem
    )
    copies[0].wait()
    widen(basis, basis_w)
    copies[1].wait()
    compress(halves, compressed)
    copies[2].wait()
    scale_w[...] = jnp.zeros((32, 128), F32)

    def outer(blk, _):
        acc = weighted(
            8, 16, 16,
            lambda i, group, u: basis_w[u * 8 + blk, i : i + 1, :],
            lambda group, u: compressed[u],
            [sketch[blk * 8 + i] for i in range(8)],
        )
        square = scale_w[...]
        for i in range(8):
            sketch[blk * 8 + i] = acc[i]
            square = square + acc[i] * acc[i]
        scale_w[...] = square
        return 0

    lax.fori_loop(0, 8, outer, 0)
    scale_w[...] = lax.rsqrt(scale_w[...] / 64 + 1e-06)

    def scaled(group, _):
        scale = scale_w[...]
        for u in range(8):
            new_basis[group * 8 + u] = sketch[group * 8 + u] * scale
        return 0

    lax.fori_loop(0, 8, scaled, 0)
    first = fetched([(new_basis, new_at)], sent)

    for tile in range(4):
        low = 8 * tile
        acc = weighted(
            8, 64, 16,
            lambda i, group, u: sketch[group * 16 + u, low + i : low + i + 1, :],
            lambda group, u: sketch[group * 16 + u, low:32, :],
            [jnp.zeros((32 - low, 128), F32)] * 8,
        )
        for i in range(8):
            gram[(low + i) * 32 + low : (low + i) * 32 + 32, :] = acc[i]
    for a in range(32):
        row = scale_w[a : a + 1, :] * (1.0 / 64)
        low = a // 8 * 8
        fresh[a, low:32, :] = gram[a * 32 + low : a * 32 + 32, :] * row
        for b in range(0, low, 8):
            fresh[a, b : b + 8, :] = gram[pl.ds(b * 32 + a, 8, stride=32), :] * row
    second = pltpu.make_async_copy(fresh, fresh_at, sent.at[1])
    second.start()
    first[0].wait()
    second.wait()


def shards(
    samples, leaf_basis_matrix, transfer, leaf_lists, leaf_coupling, parent_lists,
    parent_coupling, test_matrix,
):
    basis = leaf_basis_matrix.reshape(2048, 128)
    moves = transfer.reshape(1024, 128)
    near = leaf_coupling.reshape(4096, 128)
    above = parent_coupling.reshape(4096, 64)
    vmem = pl.BlockSpec(memory_space=pltpu.VMEM)
    anywhere = pl.BlockSpec(memory_space=pl.ANY)

    coeff = pl.pallas_call(
        coeff_kernel,
        out_shape=jax.ShapeDtypeStruct((768, 128), BF16),
        in_specs=[anywhere] * 3,
        out_specs=vmem,
        scratch_shapes=[
            pltpu.VMEM((16, 8192), BF16),
            pltpu.VMEM((2048, 128), BF16),
            pltpu.VMEM((1024, 128), BF16),
            pltpu.VMEM((256, 8, 128), F32),
            pltpu.VMEM((128, 8, 128), F32),
            pltpu.VMEM((1024, 128), F32),
            pltpu.VMEM((1024, 128), F32),
            pltpu.VMEM((32, 16, 128), F32),
            pltpu.VMEM((32, 16, 128), F32),
            pltpu.SemaphoreType.DMA((3,)),
        ],
        compiler_params=pltpu.CompilerParams(vmem_limit_bytes=62 << 20),
        name="coeff",
    )(samples, basis, moves)

    peers = lax.axis_size("cluster") * lax.axis_size("replica")
    outer = lax.ppermute(coeff, HOPS, swaps(range(1, peers - 1, 2)))
    inner = lax.ppermute(coeff, HOPS, swaps(range(0, peers - 1, 2)))

    groups = lax.axis_size("vector")
    total = pl.pallas_call(
        far_kernel,
        out_shape=jax.ShapeDtypeStruct((groups, 272, 128), BF16),
        in_specs=[anywhere] * 3 + [anywhere] * 3 + [vmem] * 3,
        out_specs=anywhere,
        scratch_shapes=[
            pltpu.VMEM((768, 128), BF16),
            pltpu.VMEM((2, 768, 128), BF16),
            pltpu.VMEM((1024, 128), BF16),
            pltpu.VMEM((4096, 128), BF16),
            pltpu.VMEM((4096, 64), BF16),
            pltpu.VMEM((512, 8, 128), F32),
            pltpu.VMEM((256, 8, 128), F32),
            pltpu.VMEM((128, 8, 128), F32),
            pltpu.VMEM((4, 32, 16, 128), F32),
            pltpu.VMEM((32, 16, 128), F32),
            pltpu.VMEM((16, 16, 128), F32),
            pltpu.VMEM((32, 16, 128), F32),
            pltpu.VMEM((2, 272, 128), BF16),
            pltpu.SemaphoreType.DMA((6,)),
            pltpu.SemaphoreType.DMA((groups,)),
        ],
        compiler_params=pltpu.CompilerParams(vmem_limit_bytes=62 << 20),
        name="far",
    )(coeff, inner, outer, moves, near, above, leaf_lists, parent_lists, test_matrix)

    mine = lax.all_to_all(total, "vector", 0, 0, tiled=True)
    product = pl.pallas_call(
        product_kernel,
        out_shape=jax.ShapeDtypeStruct((16, 8192), BF16),
        in_specs=[anywhere] * 2,
        out_specs=vmem,
        scratch_shapes=[
            pltpu.VMEM((2, 272, 128), BF16),
            pltpu.VMEM((2048, 128), BF16),
            pltpu.VMEM((256, 8, 128), F32),
            pltpu.VMEM((32, 16, 128), F32),
            pltpu.VMEM((1024, 128), F32),
            pltpu.VMEM((1024, 128), F32),
            pltpu.SemaphoreType.DMA((2,)),
        ],
        cost_estimate=pl.CostEstimate(flops=10**7, bytes_accessed=10**6, transcendentals=0),
        compiler_params=pltpu.CompilerParams(vmem_limit_bytes=24 << 20),
        name="product",
    )(total, basis)

    mine, product = lax.optimization_barrier((mine, product))
    theirs = lax.ppermute(mine, "vector", [(i, i ^ 1) for i in range(groups)])

    partial = pl.pallas_call(
        part_kernel,
        out_shape=jax.ShapeDtypeStruct((64, 32, 128), F32),
        in_specs=[anywhere] * 2,
        out_specs=anywhere,
        scratch_shapes=[
            pltpu.VMEM((groups, 272, 128), BF16),
            pltpu.VMEM((1024, 128), BF16),
            pltpu.VMEM((128, 8, 128), F32),
            pltpu.VMEM((16, 32, 128), F32),
            pltpu.VMEM((64, 32, 128), F32),
            pltpu.SemaphoreType.DMA((2,)),
            pltpu.SemaphoreType.DMA((1,)),
        ],
        cost_estimate=pl.CostEstimate(flops=10**7, bytes_accessed=10**6, transcendentals=0),
        compiler_params=pltpu.CompilerParams(vmem_limit_bytes=24 << 20),
        name="part",
    )(mine, basis)

    new_basis, fresh = pl.pallas_call(
        basis_kernel,
        out_shape=(
            jax.ShapeDtypeStruct((64, 32, 128), F32),
            jax.ShapeDtypeStruct((32, 32, 128), F32),
        ),
        in_specs=[anywhere] * 3,
        out_specs=(anywhere, anywhere),
        scratch_shapes=[
            pltpu.VMEM((groups, 272, 128), BF16),
            pltpu.VMEM((1024, 128), BF16),
            pltpu.VMEM((128, 8, 128), F32),
            pltpu.VMEM((16, 32, 128), F32),
            pltpu.VMEM((64, 32, 128), F32),
            pltpu.VMEM((32, 128), F32),
            pltpu.VMEM((1024, 128), F32),
            pltpu.VMEM((64, 32, 128), F32),
            pltpu.VMEM((32, 32, 128), F32),
            pltpu.SemaphoreType.DMA((3,)),
            pltpu.SemaphoreType.DMA((2,)),
        ],
        compiler_params=pltpu.CompilerParams(vmem_limit_bytes=24 << 20),
        name="basis",
    )(theirs, partial, basis)
    return product, new_basis, fresh


def solution(mesh):
    placed = (
        P("vector", HOPS),
        P(None, None, HOPS),
        P(None, None, HOPS),
        P(None, HOPS),
        P(None, None, None, HOPS),
        P(None, HOPS),
        P(None, None, None, HOPS),
        P("vector", None),
    )
    return jax.shard_map(
        shards,
        mesh=mesh,
        in_specs=placed,
        out_specs=(P("vector", HOPS), P(None, None, HOPS), P(None, None, HOPS)),
        check_vma=False,
    )
```

```python
import jax
import jax.numpy as jnp
from jax import lax
from jax.experimental import pallas as pl
from jax.experimental.pallas import tpu as pltpu
from jax.sharding import PartitionSpec as P

F32, BF16 = jnp.float32, jnp.bfloat16
HOPS = ("cluster", "replica")


def iota(shape, dim):
    return lax.broadcasted_iota(jnp.int32, shape, dim)


def picked(mask):
    return jnp.where(mask, 1.0, 0.0).astype(BF16)


def dot(a, b, contract=((1,), (0,))):
    return lax.dot_general(a, b, (contract, ((), ())), preferred_element_type=F32)


def widen(src, dst, step=128):
    tiles = step // 8

    def body(i, _):
        rows = src[pl.ds(pl.multiple_of(i * step, step), step), :].astype(F32)
        dst[pl.ds(i * tiles, tiles)] = rows.reshape(tiles, 8, rows.shape[-1])
        return 0

    lax.fori_loop(0, src.shape[0] // step, body, 0)


def weighted(block, steps, unroll, weight, term, init):
    def body(group, acc):
        acc = list(acc)
        for u in range(unroll):
            src = term(group, u)
            for i in range(block):
                acc[i] = acc[i] + weight(i, group, u) * src
        return tuple(acc)

    return lax.fori_loop(0, steps // unroll, body, tuple(init))


def lane_product(out, left, right_of, blocks, chunks, per, tile_of, start=None, block=8, at=0):
    rows, wide = out.shape[1:]

    def outer(blk, _):
        first = [at + blk * block + i for i in range(block)]
        init = [jnp.zeros((rows, wide), F32) if start is None else start[o] for o in first]

        def weight(i, group, u):
            c = u % 8
            return left[tile_of(first[i], group * per + u // 8), c : c + 1, :]

        acc = weighted(
            block, chunks * 8, per * 8, weight,
            lambda group, u: right_of(group * per + u // 8, u % 8), init,
        )
        for i, o in enumerate(first):
            out[o] = acc[i]
        return 0

    lax.fori_loop(0, blocks, outer, 0)


def swaps(firsts):
    return [pair for i in firsts for pair in ((i, i + 1), (i + 1, i))]


def fetched(pairs, sem):
    copies = [pltpu.make_async_copy(a, b, sem.at[i]) for i, (a, b) in enumerate(pairs)]
    for copy in copies:
        copy.start()
    return copies


def coeff_kernel(
    samples_at, basis_at, transfer_at, out,
    samples, basis, transfer, basis_w, transfer_w, xj, points, leaf, parent, sem,
):
    copies = fetched(
        [(samples_at, samples), (basis_at, basis), (transfer_at, transfer)], sem
    )
    vecs = samples.shape[0]
    row, col = iota((256, 256), 0), iota((256, 256), 1)
    spread = picked(
        (row // 64 % 2 == col // 128) & (col % 128 == 2 * (row % 64) + row // 128)
    )
    copies[0].wait()
    for j in range(64):
        xj[pl.ds(j * vecs, vecs), :] = samples[:, 128 * j : 128 * (j + 1)].astype(F32)
    for v in range(0, vecs, 2):
        pair = [xj[pl.ds(v + i, 64, stride=vecs), :] for i in range(2)]
        turned = jnp.concatenate(pair, axis=0).T
        both = dot(
            jnp.concatenate([turned[:64], turned[64:]], axis=1).astype(BF16), spread
        )
        for i in range(2):
            points[pl.ds(v + i, 64, stride=vecs), :] = both[:, 128 * i : 128 * (i + 1)]
    copies[1].wait()
    widen(basis, basis_w)
    lane_product(
        leaf, basis_w,
        lambda chunk, c: points[pl.ds(pl.multiple_of((chunk * 8 + c) * vecs, 16), vecs), :], 4, 8, 4,
        lambda r, chunk: r * 8 + chunk,
    )
    rounded = leaf[...].astype(BF16)
    out[0:512, :] = rounded.reshape(512, 128)
    leaf[...] = rounded.astype(F32)
    copies[2].wait()
    widen(transfer, transfer_w)

    def outer(blk, _):
        acc = weighted(
            8, 32, 16,
            lambda i, group, u: transfer_w[(group * 16 + u) * 4 + blk, i : i + 1, :],
            lambda group, u: leaf[group * 16 + u],
            [jnp.zeros((vecs, 128), F32)] * 8,
        )
        for i in range(8):
            parent[blk * 8 + i] = acc[i] + pltpu.roll(acc[i], 127, 1)
        return 0

    lax.fori_loop(0, 4, outer, 0)
    low = picked(iota((128, 128), 0) == 2 * iota((128, 128), 1))
    high = picked(iota((128, 128), 0) == 2 * iota((128, 128), 1) - 128)
    sums = parent[...].reshape(512, 128).astype(BF16)
    out[512:768, :] = (dot(sums[0:256], low) + dot(sums[256:512], high)).astype(BF16)


def wide_kernel(coeff, transfer, leaf_b, parent_b, own, transfer_w, coupling_w, parent_w):
    own[...] = coeff[...]
    widen(transfer, transfer_w)

    def pack(i, _):
        low = parent_b[pl.ds(pl.multiple_of(i * 128, 128), 128), :].astype(F32)
        high = parent_b[pl.ds(pl.multiple_of(2048 + i * 128, 128), 128), :].astype(F32)
        both = jnp.concatenate([low, high], axis=1)
        parent_w[pl.ds(i * 16, 16)] = both.reshape(16, 8, 128)
        return 0

    lax.fori_loop(0, 16, pack, 0)
    widen(leaf_b, coupling_w)


def far_kernel(
    own, inner, outer, transfer_w, coupling_w, parent_w, leaf_lists, parent_lists, test,
    out, source, far, pfar, wide, payload, sent,
):
    place = lax.axis_index("cluster") * lax.axis_size("replica") + lax.axis_index("replica")
    odd = lax.rem(place, 2) == 1

    def three(low, high):
        one, other = inner[low:high], outer[low:high]
        before, after = jnp.where(odd, one, other), jnp.where(odd, other, one)
        return jnp.concatenate([before, own[low:high], after], axis=1)

    first = place * 64 - 64
    none = jnp.zeros((64, 128), BF16)
    lists = jnp.concatenate([parent_lists[...], parent_lists[...]], axis=1) - first
    packed = three(512, 768)
    for k in range(4):
        index = jnp.broadcast_to(lists[k : k + 1, :], (64, 128))
        parts = []
        for m in range(3):
            hit = picked(iota((64, 128), 0) + 64 * m == index)
            parts += [jnp.concatenate(two, axis=1) for two in ((hit, none), (none, hit))]
        got = dot(packed, jnp.concatenate(parts, axis=0))
        for h in range(2):
            part = got[:, 128 * h : 128 * (h + 1)]
            source[k, 16 * h : 16 * (h + 1)] = part.reshape(16, 16, 128)

    lane_product(
        pfar, parent_w, lambda chunk, c: source[c % 4, chunk * 2 + c // 4], 2, 16, 4,
        lambda r, chunk: r * 16 + chunk,
    )
    lane = iota((256, 128), 1) // 2
    flat = pfar[...].reshape(256, 128)
    wide[0:16] = jnp.take_along_axis(flat, lane, axis=1).reshape(16, 16, 128)
    wide[16:32] = jnp.take_along_axis(flat, lane + 64, axis=1).reshape(16, 16, 128)

    first = place * 128 - 128
    rows = three(0, 512)
    for k in range(0, 4, 2):
        hits = [
            picked(
                iota((384, 128), 0)
                == jnp.broadcast_to(leaf_lists[k + i : k + i + 1, :] - first, (384, 128))
            )
            for i in range(2)
        ]
        got = dot(rows, jnp.concatenate(hits, axis=1))
        for i in range(2):
            source[k + i] = got[:, 128 * i : 128 * (i + 1)].reshape(32, 16, 128)
    lane_product(
        far, coupling_w, lambda chunk, c: source[c % 4, chunk * 2 + c // 4], 4, 16, 4,
        lambda r, chunk: r * 16 + chunk,
    )
    rows = jnp.concatenate([test[...].astype(F32), jnp.zeros((16, 128 - 32), F32)], axis=1)
    copies = []
    for h in range(2):
        lane_product(
            far, transfer_w, lambda chunk, c: wide[chunk * 8 + c], 2, 4, 4,
            lambda a, chunk: a * 4 + chunk, start=far, at=16 * h,
        )
        payload[h, 0:256, :] = far[16 * h : 16 * (h + 1)].reshape(256, 128).astype(BF16)
        payload[h, 256:272, :] = rows.astype(BF16)
        for y in range(out.shape[0] // 2):
            copy = pltpu.make_async_copy(payload.at[h], out.at[2 * y + h], sent.at[2 * y + h])
            copy.start()
            copies.append(copy)
    for copy in copies:
        copy.wait()


def product_kernel(total, basis, out, basis_w, total_w, grid, turned):
    widen(basis, basis_w)
    for h in range(2):
        rows = total[h, 0:256, :].astype(F32)
        total_w[16 * h : 16 * (h + 1)] = rows.reshape(16, 16, 128)

    def outer(blk, _):
        acc = weighted(
            8, 32, 16,
            lambda i, group, u: basis_w[(group * 16 + u) * 8 + blk, i : i + 1, :],
            lambda group, u: total_w[group * 16 + u],
            [jnp.zeros((16, 128), F32)] * 8,
        )
        for i in range(8):
            grid[pl.ds(pl.multiple_of((blk * 8 + i) * 16, 16), 16), :] = acc[i]
        return 0

    lax.fori_loop(0, 8, outer, 0)
    even = picked(iota((64, 128), 1) == 2 * iota((64, 128), 0))
    odd = picked(iota((64, 128), 1) == 2 * iota((64, 128), 0) + 1)
    none = jnp.zeros((64, 128), BF16)
    for v in range(16):
        mine = grid[pl.ds(v, 64, stride=16), :].astype(BF16)
        turned[pl.ds(v, 64, stride=16), :] = dot(even, jnp.concatenate([mine, none], axis=0), ((1,), (1,))) + dot(
            odd, jnp.concatenate([none, mine], axis=0), ((1,), (1,))
        )
    for j in range(64):
        out[:, 128 * j : 128 * (j + 1)] = turned[16 * j : 16 * (j + 1), :].astype(BF16)


def compress(halves, compressed):
    groups = range(halves.shape[0])
    tests = jnp.concatenate([halves[g, 256:272, :] for g in groups], axis=0)
    across = tests.astype(F32).T[0:32].astype(BF16)
    for a in range(16):
        rows = jnp.concatenate([halves[g, 16 * a : 16 * (a + 1), :] for g in groups], axis=0)
        compressed[a] = dot(across, rows)


def part_kernel(halves, basis, partial, basis_w, compressed):
    core = lax.rem(lax.axis_index("vector"), 2)
    widen(basis.at[pl.ds(pl.multiple_of(core * 1024, 1024), 1024)], basis_w)
    compress(halves, compressed)

    def outer(blk, _):
        acc = weighted(
            8, 16, 16,
            lambda i, group, u: basis_w[u * 8 + blk, i : i + 1, :],
            lambda group, u: compressed[u],
            [jnp.zeros((32, 128), F32)] * 8,
        )
        for i in range(8):
            partial[blk * 8 + i] = acc[i]
        return 0

    lax.fori_loop(0, 8, outer, 0)


def basis_kernel(
    halves, partial, basis, new_at, fresh_at,
    basis_w, compressed, sketch, scale_w, gram, new_basis, fresh, sent,
):
    core = 1 - lax.rem(lax.axis_index("vector"), 2)
    widen(basis.at[pl.ds(pl.multiple_of(core * 1024, 1024), 1024)], basis_w)
    compress(halves, compressed)
    scale_w[...] = jnp.zeros((32, 128), F32)

    def outer(blk, _):
        acc = weighted(
            8, 16, 16,
            lambda i, group, u: basis_w[u * 8 + blk, i : i + 1, :],
            lambda group, u: compressed[u],
            [partial[blk * 8 + i] for i in range(8)],
        )
        square = scale_w[...]
        for i in range(8):
            sketch[blk * 8 + i] = acc[i]
            square = square + acc[i] * acc[i]
        scale_w[...] = square
        return 0

    lax.fori_loop(0, 8, outer, 0)
    scale_w[...] = lax.rsqrt(scale_w[...] / 64 + 1e-06)

    def scaled(group, _):
        scale = scale_w[...]
        for u in range(8):
            new_basis[group * 8 + u] = sketch[group * 8 + u] * scale
        return 0

    lax.fori_loop(0, 8, scaled, 0)
    first = fetched([(new_basis, new_at)], sent)

    for tile in range(4):
        low = 8 * tile
        acc = weighted(
            8, 64, 16,
            lambda i, group, u: sketch[group * 16 + u, low + i : low + i + 1, :],
            lambda group, u: sketch[group * 16 + u, low:32, :],
            [jnp.zeros((32 - low, 128), F32)] * 8,
        )
        for i in range(8):
            gram[(low + i) * 32 + low : (low + i) * 32 + 32, :] = acc[i]
    for a in range(32):
        row = scale_w[a : a + 1, :] * (1.0 / 64)
        low = a // 8 * 8
        fresh[a, low:32, :] = gram[a * 32 + low : a * 32 + 32, :] * row
        for b in range(0, low, 8):
            fresh[a, b : b + 8, :] = gram[pl.ds(b * 32 + a, 8, stride=32), :] * row
    second = pltpu.make_async_copy(fresh, fresh_at, sent.at[1])
    second.start()
    first[0].wait()
    second.wait()


def shards(
    samples, leaf_basis_matrix, transfer, leaf_lists, leaf_coupling, parent_lists,
    parent_coupling, test_matrix,
):
    basis = leaf_basis_matrix.reshape(2048, 128)
    moves = transfer.reshape(1024, 128)
    near = leaf_coupling.reshape(4096, 128)
    above = parent_coupling.reshape(4096, 64)
    vmem = pl.BlockSpec(memory_space=pltpu.VMEM)
    anywhere = pl.BlockSpec(memory_space=pl.ANY)

    coeff = pl.pallas_call(
        coeff_kernel,
        out_shape=jax.ShapeDtypeStruct((768, 128), BF16),
        in_specs=[anywhere] * 3,
        out_specs=vmem,
        scratch_shapes=[
            pltpu.VMEM((16, 8192), BF16),
            pltpu.VMEM((2048, 128), BF16),
            pltpu.VMEM((1024, 128), BF16),
            pltpu.VMEM((256, 8, 128), F32),
            pltpu.VMEM((128, 8, 128), F32),
            pltpu.VMEM((1024, 128), F32),
            pltpu.VMEM((1024, 128), F32),
            pltpu.VMEM((32, 16, 128), F32),
            pltpu.VMEM((32, 16, 128), F32),
            pltpu.SemaphoreType.DMA((3,)),
        ],
        compiler_params=pltpu.CompilerParams(vmem_limit_bytes=62 << 20),
        name="coeff",
    )(samples, basis, moves)

    peers = lax.axis_size("cluster") * lax.axis_size("replica")
    outer = lax.ppermute(coeff, HOPS, swaps(range(1, peers - 1, 2)))
    inner = lax.ppermute(coeff, HOPS, swaps(range(0, peers - 1, 2)))

    groups = lax.axis_size("vector")
    own, transfer_w, coupling_w, parent_w = pl.pallas_call(
        wide_kernel,
        out_shape=(
            jax.ShapeDtypeStruct((768, 128), BF16),
            jax.ShapeDtypeStruct((128, 8, 128), F32),
            jax.ShapeDtypeStruct((512, 8, 128), F32),
            jax.ShapeDtypeStruct((256, 8, 128), F32),
        ),
        in_specs=[vmem] * 4,
        out_specs=(vmem,) * 4,
        cost_estimate=pl.CostEstimate(flops=10**7, bytes_accessed=10**6, transcendentals=0),
        compiler_params=pltpu.CompilerParams(vmem_limit_bytes=24 << 20),
        name="wide",
    )(coeff, moves, near, above)

    total = pl.pallas_call(
        far_kernel,
        out_shape=jax.ShapeDtypeStruct((groups, 272, 128), BF16),
        in_specs=[vmem] * 9,
        out_specs=anywhere,
        scratch_shapes=[
            pltpu.VMEM((4, 32, 16, 128), F32),
            pltpu.VMEM((32, 16, 128), F32),
            pltpu.VMEM((16, 16, 128), F32),
            pltpu.VMEM((32, 16, 128), F32),
            pltpu.VMEM((2, 272, 128), BF16),
            pltpu.SemaphoreType.DMA((groups,)),
        ],
        compiler_params=pltpu.CompilerParams(vmem_limit_bytes=24 << 20),
        name="far",
    )(own, inner, outer, transfer_w, coupling_w, parent_w, leaf_lists, parent_lists, test_matrix)

    mine = lax.all_to_all(total, "vector", 0, 0, tiled=True)
    product = pl.pallas_call(
        product_kernel,
        out_shape=jax.ShapeDtypeStruct((16, 8192), BF16),
        in_specs=[vmem] * 2,
        out_specs=vmem,
        scratch_shapes=[
            pltpu.VMEM((256, 8, 128), F32),
            pltpu.VMEM((32, 16, 128), F32),
            pltpu.VMEM((1024, 128), F32),
            pltpu.VMEM((1024, 128), F32),
        ],
        cost_estimate=pl.CostEstimate(flops=10**7, bytes_accessed=10**6, transcendentals=0),
        compiler_params=pltpu.CompilerParams(vmem_limit_bytes=24 << 20),
        name="product",
    )(total, basis)

    mine, product = lax.optimization_barrier((mine, product))
    theirs = lax.ppermute(mine, "vector", [(i, i ^ 1) for i in range(groups)])

    partial = pl.pallas_call(
        part_kernel,
        out_shape=jax.ShapeDtypeStruct((64, 32, 128), F32),
        in_specs=[vmem] * 2,
        out_specs=vmem,
        scratch_shapes=[
            pltpu.VMEM((128, 8, 128), F32),
            pltpu.VMEM((16, 32, 128), F32),
        ],
        cost_estimate=pl.CostEstimate(flops=10**7, bytes_accessed=10**6, transcendentals=0),
        compiler_params=pltpu.CompilerParams(vmem_limit_bytes=24 << 20),
        name="part",
    )(mine, basis)

    new_basis, fresh = pl.pallas_call(
        basis_kernel,
        out_shape=(
            jax.ShapeDtypeStruct((64, 32, 128), F32),
            jax.ShapeDtypeStruct((32, 32, 128), F32),
        ),
        in_specs=[vmem] * 3,
        out_specs=(anywhere, anywhere),
        scratch_shapes=[
            pltpu.VMEM((128, 8, 128), F32),
            pltpu.VMEM((16, 32, 128), F32),
            pltpu.VMEM((64, 32, 128), F32),
            pltpu.VMEM((32, 128), F32),
            pltpu.VMEM((1024, 128), F32),
            pltpu.VMEM((64, 32, 128), F32),
            pltpu.VMEM((32, 32, 128), F32),
            pltpu.SemaphoreType.DMA((2,)),
        ],
        compiler_params=pltpu.CompilerParams(vmem_limit_bytes=24 << 20),
        name="basis",
    )(theirs, partial, basis)
    return product, new_basis, fresh


def solution(mesh):
    placed = (
        P("vector", HOPS),
        P(None, None, HOPS),
        P(None, None, HOPS),
        P(None, HOPS),
        P(None, None, None, HOPS),
        P(None, HOPS),
        P(None, None, None, HOPS),
        P("vector", None),
    )
    return jax.shard_map(
        shards,
        mesh=mesh,
        in_specs=placed,
        out_specs=(P("vector", HOPS), P(None, None, HOPS), P(None, None, HOPS)),
        check_vma=False,
    )
```

```python
import jax
import jax.numpy as jnp
from jax import lax
from jax.experimental import pallas as pl
from jax.experimental.pallas import tpu as pltpu
from jax.sharding import PartitionSpec as P

F32, BF16 = jnp.float32, jnp.bfloat16
HOPS = ("cluster", "replica")


def iota(shape, dim):
    return lax.broadcasted_iota(jnp.int32, shape, dim)


def picked(mask):
    return jnp.where(mask, 1.0, 0.0).astype(BF16)


def dot(a, b, contract=((1,), (0,))):
    return lax.dot_general(a, b, (contract, ((), ())), preferred_element_type=F32)


def widen(src, dst, step=128):
    tiles = step // 8

    def body(i, _):
        rows = src[pl.ds(pl.multiple_of(i * step, step), step), :].astype(F32)
        dst[pl.ds(i * tiles, tiles)] = rows.reshape(tiles, 8, rows.shape[-1])
        return 0

    lax.fori_loop(0, src.shape[0] // step, body, 0)


def weighted(block, steps, unroll, weight, term, init):
    def body(group, acc):
        acc = list(acc)
        for u in range(unroll):
            src = term(group, u)
            for i in range(block):
                acc[i] = acc[i] + weight(i, group, u) * src
        return tuple(acc)

    return lax.fori_loop(0, steps // unroll, body, tuple(init))


def lane_product(out, left, right_of, blocks, chunks, per, tile_of, start=None, block=8, at=0):
    rows, wide = out.shape[1:]

    def outer(blk, _):
        first = [at + blk * block + i for i in range(block)]
        init = [jnp.zeros((rows, wide), F32) if start is None else start[o] for o in first]

        def weight(i, group, u):
            c = u % 8
            return left[tile_of(first[i], group * per + u // 8), c : c + 1, :]

        acc = weighted(
            block, chunks * 8, per * 8, weight,
            lambda group, u: right_of(group * per + u // 8, u % 8), init,
        )
        for i, o in enumerate(first):
            out[o] = acc[i]
        return 0

    lax.fori_loop(0, blocks, outer, 0)


def swaps(firsts):
    return [pair for i in firsts for pair in ((i, i + 1), (i + 1, i))]


def fetched(pairs, sem):
    copies = [pltpu.make_async_copy(a, b, sem.at[i]) for i, (a, b) in enumerate(pairs)]
    for copy in copies:
        copy.start()
    return copies


def coeff_kernel(
    samples_at, basis_at, transfer_at, out,
    samples, basis, transfer, basis_w, transfer_w, xj, points, leaf, parent, sem,
):
    copies = fetched(
        [(samples_at, samples), (basis_at, basis), (transfer_at, transfer)], sem
    )
    vecs = samples.shape[0]
    row, col = iota((256, 256), 0), iota((256, 256), 1)
    spread = picked(
        (row // 64 % 2 == col // 128) & (col % 128 == 2 * (row % 64) + row // 128)
    )
    copies[0].wait()
    for j in range(64):
        xj[pl.ds(j * vecs, vecs), :] = samples[:, 128 * j : 128 * (j + 1)].astype(F32)
    for v in range(0, vecs, 2):
        pair = [xj[pl.ds(v + i, 64, stride=vecs), :] for i in range(2)]
        turned = jnp.concatenate(pair, axis=0).T
        both = dot(
            jnp.concatenate([turned[:64], turned[64:]], axis=1).astype(BF16), spread
        )
        for i in range(2):
            points[pl.ds(v + i, 64, stride=vecs), :] = both[:, 128 * i : 128 * (i + 1)]
    copies[1].wait()
    widen(basis, basis_w)
    lane_product(
        leaf, basis_w,
        lambda chunk, c: points[pl.ds(pl.multiple_of((chunk * 8 + c) * vecs, 16), vecs), :], 4, 8, 4,
        lambda r, chunk: r * 8 + chunk,
    )
    rounded = leaf[...].astype(BF16)
    out[0:512, :] = rounded.reshape(512, 128)
    leaf[...] = rounded.astype(F32)
    copies[2].wait()
    widen(transfer, transfer_w)

    def outer(blk, _):
        acc = weighted(
            8, 32, 16,
            lambda i, group, u: transfer_w[(group * 16 + u) * 4 + blk, i : i + 1, :],
            lambda group, u: leaf[group * 16 + u],
            [jnp.zeros((vecs, 128), F32)] * 8,
        )
        for i in range(8):
            parent[blk * 8 + i] = acc[i] + pltpu.roll(acc[i], 127, 1)
        return 0

    lax.fori_loop(0, 4, outer, 0)
    low = picked(iota((128, 128), 0) == 2 * iota((128, 128), 1))
    high = picked(iota((128, 128), 0) == 2 * iota((128, 128), 1) - 128)
    sums = parent[...].reshape(512, 128).astype(BF16)
    out[512:768, :] = (dot(sums[0:256], low) + dot(sums[256:512], high)).astype(BF16)


def wide_kernel(coeff, transfer, leaf_b, parent_b, own, transfer_w, coupling_w, parent_w):
    own[...] = coeff[...]
    widen(transfer, transfer_w)

    def pack(i, _):
        low = parent_b[pl.ds(pl.multiple_of(i * 128, 128), 128), :].astype(F32)
        high = parent_b[pl.ds(pl.multiple_of(2048 + i * 128, 128), 128), :].astype(F32)
        both = jnp.concatenate([low, high], axis=1)
        parent_w[pl.ds(i * 16, 16)] = both.reshape(16, 8, 128)
        return 0

    lax.fori_loop(0, 16, pack, 0)
    widen(leaf_b, coupling_w)


def far_kernel(
    own, inner, outer, transfer_w, coupling_w, parent_w, leaf_lists, parent_lists, test,
    out, source, far, pfar, wide, payload, sent,
):
    place = lax.axis_index("cluster") * lax.axis_size("replica") + lax.axis_index("replica")
    odd = lax.rem(place, 2) == 1

    def three(low, high):
        one, other = inner[low:high], outer[low:high]
        before, after = jnp.where(odd, one, other), jnp.where(odd, other, one)
        return jnp.concatenate([before, own[low:high], after], axis=1)

    first = place * 64 - 64
    none = jnp.zeros((64, 128), BF16)
    lists = jnp.concatenate([parent_lists[...], parent_lists[...]], axis=1) - first
    packed = three(512, 768)
    for k in range(4):
        index = jnp.broadcast_to(lists[k : k + 1, :], (64, 128))
        parts = []
        for m in range(3):
            hit = picked(iota((64, 128), 0) + 64 * m == index)
            parts += [jnp.concatenate(two, axis=1) for two in ((hit, none), (none, hit))]
        got = dot(packed, jnp.concatenate(parts, axis=0))
        for h in range(2):
            part = got[:, 128 * h : 128 * (h + 1)]
            source[k, 16 * h : 16 * (h + 1)] = part.reshape(16, 16, 128)

    lane_product(
        pfar, parent_w, lambda chunk, c: source[c % 4, chunk * 2 + c // 4], 2, 16, 4,
        lambda r, chunk: r * 16 + chunk,
    )
    lane = iota((256, 128), 1) // 2
    flat = pfar[...].reshape(256, 128)
    wide[0:16] = jnp.take_along_axis(flat, lane, axis=1).reshape(16, 16, 128)
    wide[16:32] = jnp.take_along_axis(flat, lane + 64, axis=1).reshape(16, 16, 128)

    first = place * 128 - 128
    rows = three(0, 512)
    for k in range(0, 4, 2):
        hits = [
            picked(
                iota((384, 128), 0)
                == jnp.broadcast_to(leaf_lists[k + i : k + i + 1, :] - first, (384, 128))
            )
            for i in range(2)
        ]
        got = dot(rows, jnp.concatenate(hits, axis=1))
        for i in range(2):
            source[k + i] = got[:, 128 * i : 128 * (i + 1)].reshape(32, 16, 128)
    lane_product(
        far, coupling_w, lambda chunk, c: source[c % 4, chunk * 2 + c // 4], 4, 16, 4,
        lambda r, chunk: r * 16 + chunk,
    )
    rows = jnp.concatenate([test[...].astype(F32), jnp.zeros((16, 128 - 32), F32)], axis=1)
    payload[512:528, :] = rows.astype(BF16)
    copies = []
    peers = out.shape[0]
    for h in range(2):
        lane_product(
            far, transfer_w, lambda chunk, c: wide[chunk * 8 + c], 2, 4, 4,
            lambda a, chunk: a * 4 + chunk, start=far, at=16 * h,
        )
        low = 256 * h
        payload[low : low + 256, :] = far[16 * h : 16 * (h + 1)].reshape(256, 128).astype(BF16)
        sent_rows = pl.ds(low, 256 if h == 0 else 272)
        for y in range(peers):
            copy = pltpu.make_async_copy(
                payload.at[sent_rows], out.at[y, sent_rows], sent.at[peers * h + y]
            )
            copy.start()
            copies.append(copy)
    for copy in copies:
        copy.wait()


def product_kernel(total, basis, out, basis_w, total_w, grid, turned):
    widen(basis, basis_w)
    total_w[...] = total[0, 0:512, :].astype(F32).reshape(32, 16, 128)

    def outer(blk, _):
        acc = weighted(
            8, 32, 16,
            lambda i, group, u: basis_w[(group * 16 + u) * 8 + blk, i : i + 1, :],
            lambda group, u: total_w[group * 16 + u],
            [jnp.zeros((16, 128), F32)] * 8,
        )
        for i in range(8):
            grid[pl.ds(pl.multiple_of((blk * 8 + i) * 16, 16), 16), :] = acc[i]
        return 0

    lax.fori_loop(0, 8, outer, 0)
    even = picked(iota((64, 128), 1) == 2 * iota((64, 128), 0))
    odd = picked(iota((64, 128), 1) == 2 * iota((64, 128), 0) + 1)
    none = jnp.zeros((64, 128), BF16)
    for v in range(16):
        mine = grid[pl.ds(v, 64, stride=16), :].astype(BF16)
        turned[pl.ds(v, 64, stride=16), :] = dot(even, jnp.concatenate([mine, none], axis=0), ((1,), (1,))) + dot(
            odd, jnp.concatenate([none, mine], axis=0), ((1,), (1,))
        )
    for j in range(64):
        out[:, 128 * j : 128 * (j + 1)] = turned[16 * j : 16 * (j + 1), :].astype(BF16)


def compressed_ranks(totals):
    groups = range(totals.shape[0])
    tests = jnp.concatenate([totals[g, 512:528, :] for g in groups], axis=0)
    across = tests.astype(F32).T[0:32].astype(BF16)
    for a in range(32):
        rows = jnp.concatenate([totals[g, 16 * a : 16 * (a + 1), :] for g in groups], axis=0)
        yield a, dot(across, rows)


def part_kernel(mine, partial):
    for a, part in compressed_ranks(mine):
        partial[a] = part


def basis_kernel(
    theirs, partial, basis, new_at, fresh_at,
    basis_w, compressed, sketch, scale_w, gram, new_basis, fresh, sent,
):
    widen(basis, basis_w)
    for a, part in compressed_ranks(theirs):
        compressed[a] = partial[a] + part
    scale_w[...] = jnp.zeros((32, 128), F32)

    def outer(blk, _):
        acc = weighted(
            8, 32, 16,
            lambda i, group, u: basis_w[(group * 16 + u) * 8 + blk, i : i + 1, :],
            lambda group, u: compressed[group * 16 + u],
            [jnp.zeros((32, 128), F32)] * 8,
        )
        square = scale_w[...]
        for i in range(8):
            sketch[blk * 8 + i] = acc[i]
            square = square + acc[i] * acc[i]
        scale_w[...] = square
        return 0

    lax.fori_loop(0, 8, outer, 0)
    scale_w[...] = lax.rsqrt(scale_w[...] / 64 + 1e-06)

    def scaled(group, _):
        scale = scale_w[...]
        for u in range(8):
            new_basis[group * 8 + u] = sketch[group * 8 + u] * scale
        return 0

    lax.fori_loop(0, 8, scaled, 0)
    copies = fetched([(new_basis, new_at)], sent)

    for tile in range(4):
        low = 8 * tile
        acc = weighted(
            8, 64, 16,
            lambda i, group, u: sketch[group * 16 + u, low + i : low + i + 1, :],
            lambda group, u: sketch[group * 16 + u, low:32, :],
            [jnp.zeros((32 - low, 128), F32)] * 8,
        )
        for i in range(8):
            a = low + i
            row = scale_w[a : a + 1, :] * (1.0 / 64)
            gram[a * 32 + low : a * 32 + 32, :] = acc[i]
            fresh[a, low:32, :] = acc[i] * row
            for b in range(0, low, 8):
                fresh[a, b : b + 8, :] = gram[pl.ds(b * 32 + a, 8, stride=32), :] * row
        ranks = pl.ds(low, 8)
        copy = pltpu.make_async_copy(fresh.at[ranks], fresh_at.at[ranks], sent.at[1 + tile])
        copy.start()
        copies.append(copy)
    for copy in copies:
        copy.wait()


def shards(
    samples, leaf_basis_matrix, transfer, leaf_lists, leaf_coupling, parent_lists,
    parent_coupling, test_matrix,
):
    basis = leaf_basis_matrix.reshape(2048, 128)
    moves = transfer.reshape(1024, 128)
    near = leaf_coupling.reshape(4096, 128)
    above = parent_coupling.reshape(4096, 64)
    vmem = pl.BlockSpec(memory_space=pltpu.VMEM)
    anywhere = pl.BlockSpec(memory_space=pl.ANY)

    coeff = pl.pallas_call(
        coeff_kernel,
        out_shape=jax.ShapeDtypeStruct((768, 128), BF16),
        in_specs=[anywhere] * 3,
        out_specs=vmem,
        scratch_shapes=[
            pltpu.VMEM((16, 8192), BF16),
            pltpu.VMEM((2048, 128), BF16),
            pltpu.VMEM((1024, 128), BF16),
            pltpu.VMEM((256, 8, 128), F32),
            pltpu.VMEM((128, 8, 128), F32),
            pltpu.VMEM((1024, 128), F32),
            pltpu.VMEM((1024, 128), F32),
            pltpu.VMEM((32, 16, 128), F32),
            pltpu.VMEM((32, 16, 128), F32),
            pltpu.SemaphoreType.DMA((3,)),
        ],
        compiler_params=pltpu.CompilerParams(vmem_limit_bytes=62 << 20),
        name="coeff",
    )(samples, basis, moves)

    peers = lax.axis_size("cluster") * lax.axis_size("replica")
    outer = lax.ppermute(coeff, HOPS, swaps(range(1, peers - 1, 2)))
    inner = lax.ppermute(coeff, HOPS, swaps(range(0, peers - 1, 2)))

    groups = lax.axis_size("vector")
    half = groups // 2
    own, transfer_w, coupling_w, parent_w = pl.pallas_call(
        wide_kernel,
        out_shape=(
            jax.ShapeDtypeStruct((768, 128), BF16),
            jax.ShapeDtypeStruct((128, 8, 128), F32),
            jax.ShapeDtypeStruct((512, 8, 128), F32),
            jax.ShapeDtypeStruct((256, 8, 128), F32),
        ),
        in_specs=[vmem] * 4,
        out_specs=(vmem,) * 4,
        cost_estimate=pl.CostEstimate(flops=10**7, bytes_accessed=10**6, transcendentals=0),
        compiler_params=pltpu.CompilerParams(vmem_limit_bytes=24 << 20),
        name="wide",
    )(coeff, moves, near, above)

    total = pl.pallas_call(
        far_kernel,
        out_shape=jax.ShapeDtypeStruct((half, 528, 128), BF16),
        in_specs=[vmem] * 9,
        out_specs=anywhere,
        scratch_shapes=[
            pltpu.VMEM((4, 32, 16, 128), F32),
            pltpu.VMEM((32, 16, 128), F32),
            pltpu.VMEM((16, 16, 128), F32),
            pltpu.VMEM((32, 16, 128), F32),
            pltpu.VMEM((528, 128), BF16),
            pltpu.SemaphoreType.DMA((groups,)),
        ],
        compiler_params=pltpu.CompilerParams(vmem_limit_bytes=24 << 20),
        name="far",
    )(own, inner, outer, transfer_w, coupling_w, parent_w, leaf_lists, parent_lists, test_matrix)

    cores = [[2 * y + core for y in range(half)] for core in range(2)]
    mine = lax.all_to_all(total, "vector", 0, 0, tiled=True, axis_index_groups=cores)

    product = pl.pallas_call(
        product_kernel,
        out_shape=jax.ShapeDtypeStruct((16, 8192), BF16),
        in_specs=[vmem] * 2,
        out_specs=vmem,
        scratch_shapes=[
            pltpu.VMEM((256, 8, 128), F32),
            pltpu.VMEM((32, 16, 128), F32),
            pltpu.VMEM((1024, 128), F32),
            pltpu.VMEM((1024, 128), F32),
        ],
        cost_estimate=pl.CostEstimate(flops=10**7, bytes_accessed=10**6, transcendentals=0),
        compiler_params=pltpu.CompilerParams(vmem_limit_bytes=24 << 20),
        name="product",
    )(total, basis)

    mine, product = lax.optimization_barrier((mine, product))
    theirs = lax.ppermute(mine, "vector", [(i, i ^ 1) for i in range(groups)])

    partial = pl.pallas_call(
        part_kernel,
        out_shape=jax.ShapeDtypeStruct((32, 32, 128), F32),
        in_specs=[vmem],
        out_specs=vmem,
        cost_estimate=pl.CostEstimate(flops=10**7, bytes_accessed=10**6, transcendentals=0),
        compiler_params=pltpu.CompilerParams(vmem_limit_bytes=24 << 20),
        name="part",
    )(mine)

    new_basis, fresh = pl.pallas_call(
        basis_kernel,
        out_shape=(
            jax.ShapeDtypeStruct((64, 32, 128), F32),
            jax.ShapeDtypeStruct((32, 32, 128), F32),
        ),
        in_specs=[vmem] * 3,
        out_specs=(anywhere, anywhere),
        scratch_shapes=[
            pltpu.VMEM((256, 8, 128), F32),
            pltpu.VMEM((32, 32, 128), F32),
            pltpu.VMEM((64, 32, 128), F32),
            pltpu.VMEM((32, 128), F32),
            pltpu.VMEM((1024, 128), F32),
            pltpu.VMEM((64, 32, 128), F32),
            pltpu.VMEM((32, 32, 128), F32),
            pltpu.SemaphoreType.DMA((5,)),
        ],
        compiler_params=pltpu.CompilerParams(vmem_limit_bytes=24 << 20),
        name="basis",
    )(theirs, partial, basis)
    return product, new_basis, fresh


def solution(mesh):
    placed = (
        P("vector", HOPS),
        P(None, None, HOPS),
        P(None, None, HOPS),
        P(None, HOPS),
        P(None, None, None, HOPS),
        P(None, HOPS),
        P(None, None, None, HOPS),
        P("vector", None),
    )
    return jax.shard_map(
        shards,
        mesh=mesh,
        in_specs=placed,
        out_specs=(P("vector", HOPS), P(None, None, HOPS), P(None, None, HOPS)),
        check_vma=False,
    )
```

```python
import jax
import jax.numpy as jnp
from jax import lax
from jax.experimental import pallas as pl
from jax.experimental.pallas import tpu as pltpu
from jax.sharding import PartitionSpec as P

F32, BF16 = jnp.float32, jnp.bfloat16
HOPS = ("cluster", "replica")


def iota(shape, dim):
    return lax.broadcasted_iota(jnp.int32, shape, dim)


def picked(mask):
    return jnp.where(mask, 1.0, 0.0).astype(BF16)


def dot(a, b, contract=((1,), (0,))):
    return lax.dot_general(a, b, (contract, ((), ())), preferred_element_type=F32)


def widen(src, dst, step=128):
    tiles = step // 8

    def body(i, _):
        rows = src[pl.ds(pl.multiple_of(i * step, step), step), :].astype(F32)
        dst[pl.ds(i * tiles, tiles)] = rows.reshape(tiles, 8, rows.shape[-1])
        return 0

    lax.fori_loop(0, src.shape[0] // step, body, 0)


def weighted(block, steps, unroll, weight, term, init):
    def body(group, acc):
        acc = list(acc)
        for u in range(unroll):
            src = term(group, u)
            for i in range(block):
                acc[i] = acc[i] + weight(i, group, u) * src
        return tuple(acc)

    return lax.fori_loop(0, steps // unroll, body, tuple(init))


def lane_product(out, left, right_of, blocks, chunks, per, tile_of, start=None, block=8, at=0):
    rows, wide = out.shape[1:]

    def outer(blk, _):
        first = [at + blk * block + i for i in range(block)]
        init = [jnp.zeros((rows, wide), F32) if start is None else start[o] for o in first]

        def weight(i, group, u):
            c = u % 8
            return left[tile_of(first[i], group * per + u // 8), c : c + 1, :]

        acc = weighted(
            block, chunks * 8, per * 8, weight,
            lambda group, u: right_of(group * per + u // 8, u % 8), init,
        )
        for i, o in enumerate(first):
            out[o] = acc[i]
        return 0

    lax.fori_loop(0, blocks, outer, 0)


def swaps(firsts):
    return [pair for i in firsts for pair in ((i, i + 1), (i + 1, i))]


def fetched(pairs, sem):
    copies = [pltpu.make_async_copy(a, b, sem.at[i]) for i, (a, b) in enumerate(pairs)]
    for copy in copies:
        copy.start()
    return copies


def coeff_kernel(
    samples_at, basis_at, transfer_at, out_at,
    samples, basis, transfer, basis_w, transfer_w, xj, points, leaf, parent, out, sem, sent,
):
    copies = fetched(
        [(samples_at, samples), (basis_at, basis), (transfer_at, transfer)], sem
    )
    vecs = samples.shape[0]
    row, col = iota((256, 256), 0), iota((256, 256), 1)
    spread = picked(
        (row // 64 % 2 == col // 128) & (col % 128 == 2 * (row % 64) + row // 128)
    )
    copies[0].wait()
    for j in range(64):
        xj[pl.ds(j * vecs, vecs), :] = samples[:, 128 * j : 128 * (j + 1)].astype(F32)
    for v in range(0, vecs, 2):
        pair = [xj[pl.ds(v + i, 64, stride=vecs), :] for i in range(2)]
        turned = jnp.concatenate(pair, axis=0).T
        both = dot(
            jnp.concatenate([turned[:64], turned[64:]], axis=1).astype(BF16), spread
        )
        for i in range(2):
            points[pl.ds(v + i, 64, stride=vecs), :] = both[:, 128 * i : 128 * (i + 1)]
    copies[1].wait()
    widen(basis, basis_w)
    lane_product(
        leaf, basis_w,
        lambda chunk, c: points[pl.ds(pl.multiple_of((chunk * 8 + c) * vecs, 16), vecs), :], 4, 8, 4,
        lambda r, chunk: r * 8 + chunk,
    )
    rounded = leaf[...].astype(BF16)
    out[0:512, :] = rounded.reshape(512, 128)
    first = pltpu.make_async_copy(out.at[0:512], out_at.at[0:512], sent.at[0])
    first.start()
    leaf[...] = rounded.astype(F32)
    copies[2].wait()
    widen(transfer, transfer_w)

    def outer(blk, _):
        acc = weighted(
            8, 32, 16,
            lambda i, group, u: transfer_w[(group * 16 + u) * 4 + blk, i : i + 1, :],
            lambda group, u: leaf[group * 16 + u],
            [jnp.zeros((vecs, 128), F32)] * 8,
        )
        for i in range(8):
            parent[blk * 8 + i] = acc[i] + pltpu.roll(acc[i], 127, 1)
        return 0

    lax.fori_loop(0, 4, outer, 0)
    low = picked(iota((128, 128), 0) == 2 * iota((128, 128), 1))
    high = picked(iota((128, 128), 0) == 2 * iota((128, 128), 1) - 128)
    sums = parent[...].reshape(512, 128).astype(BF16)
    out[512:768, :] = (dot(sums[0:256], low) + dot(sums[256:512], high)).astype(BF16)
    second = pltpu.make_async_copy(out.at[512:768], out_at.at[512:768], sent.at[1])
    second.start()
    first.wait()
    second.wait()


def wide_kernel(coeff, transfer, leaf_b, parent_b, own, transfer_w, coupling_w, parent_w):
    own[...] = coeff[...]
    widen(transfer, transfer_w)

    def pack(i, _):
        low = parent_b[pl.ds(pl.multiple_of(i * 128, 128), 128), :].astype(F32)
        high = parent_b[pl.ds(pl.multiple_of(2048 + i * 128, 128), 128), :].astype(F32)
        both = jnp.concatenate([low, high], axis=1)
        parent_w[pl.ds(i * 16, 16)] = both.reshape(16, 8, 128)
        return 0

    lax.fori_loop(0, 16, pack, 0)
    widen(leaf_b, coupling_w)


def far_kernel(
    own, inner, outer, transfer_w, coupling_w, parent_w, leaf_lists, parent_lists, test,
    out, source, far, pfar, wide, payload, sent,
):
    place = lax.axis_index("cluster") * lax.axis_size("replica") + lax.axis_index("replica")
    odd = lax.rem(place, 2) == 1

    def three(low, high):
        one, other = inner[low:high], outer[low:high]
        before, after = jnp.where(odd, one, other), jnp.where(odd, other, one)
        return jnp.concatenate([before, own[low:high], after], axis=1)

    first = place * 64 - 64
    none = jnp.zeros((64, 128), BF16)
    lists = jnp.concatenate([parent_lists[...], parent_lists[...]], axis=1) - first
    packed = three(512, 768)
    for k in range(4):
        index = jnp.broadcast_to(lists[k : k + 1, :], (64, 128))
        parts = []
        for m in range(3):
            hit = picked(iota((64, 128), 0) + 64 * m == index)
            parts += [jnp.concatenate(two, axis=1) for two in ((hit, none), (none, hit))]
        got = dot(packed, jnp.concatenate(parts, axis=0))
        for h in range(2):
            part = got[:, 128 * h : 128 * (h + 1)]
            source[k, 16 * h : 16 * (h + 1)] = part.reshape(16, 16, 128)

    lane_product(
        pfar, parent_w, lambda chunk, c: source[c % 4, chunk * 2 + c // 4], 2, 16, 4,
        lambda r, chunk: r * 16 + chunk,
    )
    lane = iota((256, 128), 1) // 2
    flat = pfar[...].reshape(256, 128)
    wide[0:16] = jnp.take_along_axis(flat, lane, axis=1).reshape(16, 16, 128)
    wide[16:32] = jnp.take_along_axis(flat, lane + 64, axis=1).reshape(16, 16, 128)

    first = place * 128 - 128
    rows = three(0, 512)
    for k in range(0, 4, 2):
        hits = [
            picked(
                iota((384, 128), 0)
                == jnp.broadcast_to(leaf_lists[k + i : k + i + 1, :] - first, (384, 128))
            )
            for i in range(2)
        ]
        got = dot(rows, jnp.concatenate(hits, axis=1))
        for i in range(2):
            source[k + i] = got[:, 128 * i : 128 * (i + 1)].reshape(32, 16, 128)
    lane_product(
        far, coupling_w, lambda chunk, c: source[c % 4, chunk * 2 + c // 4], 4, 16, 4,
        lambda r, chunk: r * 16 + chunk,
    )
    rows = jnp.concatenate([test[...].astype(F32), jnp.zeros((16, 128 - 32), F32)], axis=1)
    payload[512:528, :] = rows.astype(BF16)
    copies = []
    peers = out.shape[0]
    for h in range(2):
        lane_product(
            far, transfer_w, lambda chunk, c: wide[chunk * 8 + c], 2, 4, 4,
            lambda a, chunk: a * 4 + chunk, start=far, at=16 * h,
        )
        low = 256 * h
        payload[low : low + 256, :] = far[16 * h : 16 * (h + 1)].reshape(256, 128).astype(BF16)
        sent_rows = pl.ds(low, 256 if h == 0 else 272)
        for y in range(peers):
            copy = pltpu.make_async_copy(
                payload.at[sent_rows], out.at[y, sent_rows], sent.at[peers * h + y]
            )
            copy.start()
            copies.append(copy)
    for copy in copies:
        copy.wait()


def product_kernel(total, basis, out, basis_w, total_w, grid, turned):
    widen(basis, basis_w)
    total_w[...] = total[0, 0:512, :].astype(F32).reshape(32, 16, 128)

    def outer(blk, _):
        acc = weighted(
            8, 32, 16,
            lambda i, group, u: basis_w[(group * 16 + u) * 8 + blk, i : i + 1, :],
            lambda group, u: total_w[group * 16 + u],
            [jnp.zeros((16, 128), F32)] * 8,
        )
        for i in range(8):
            grid[pl.ds(pl.multiple_of((blk * 8 + i) * 16, 16), 16), :] = acc[i]
        return 0

    lax.fori_loop(0, 8, outer, 0)
    even = picked(iota((64, 128), 1) == 2 * iota((64, 128), 0))
    odd = picked(iota((64, 128), 1) == 2 * iota((64, 128), 0) + 1)
    none = jnp.zeros((64, 128), BF16)
    for v in range(16):
        mine = grid[pl.ds(v, 64, stride=16), :].astype(BF16)
        turned[pl.ds(v, 64, stride=16), :] = dot(even, jnp.concatenate([mine, none], axis=0), ((1,), (1,))) + dot(
            odd, jnp.concatenate([none, mine], axis=0), ((1,), (1,))
        )
    for j in range(64):
        out[:, 128 * j : 128 * (j + 1)] = turned[16 * j : 16 * (j + 1), :].astype(BF16)


def part_kernel(totals, partial):
    groups = range(totals.shape[0])
    tests = jnp.concatenate([totals[g, 512:528, :] for g in groups], axis=0)
    across = tests.astype(F32).T[0:32].astype(BF16)
    for a in range(32):
        rows = jnp.concatenate([totals[g, 16 * a : 16 * (a + 1), :] for g in groups], axis=0)
        partial[32 * a : 32 * (a + 1), :] = dot(across, rows).astype(BF16)


def basis_kernel(
    mine, theirs, basis, new_at, fresh_at,
    basis_w, compressed, sketch, scale_w, gram, new_basis, fresh, sent,
):
    widen(basis, basis_w)
    for a in range(0, 1024, 128):
        both = mine[a : a + 128, :].astype(F32) + theirs[a : a + 128, :].astype(F32)
        compressed[a // 32 : a // 32 + 4] = both.reshape(4, 32, 128)
    scale_w[...] = jnp.zeros((32, 128), F32)

    def outer(blk, _):
        acc = weighted(
            8, 32, 16,
            lambda i, group, u: basis_w[(group * 16 + u) * 8 + blk, i : i + 1, :],
            lambda group, u: compressed[group * 16 + u],
            [jnp.zeros((32, 128), F32)] * 8,
        )
        square = scale_w[...]
        for i in range(8):
            sketch[blk * 8 + i] = acc[i]
            square = square + acc[i] * acc[i]
        scale_w[...] = square
        return 0

    lax.fori_loop(0, 8, outer, 0)
    scale_w[...] = lax.rsqrt(scale_w[...] / 64 + 1e-06)

    def scaled(group, _):
        scale = scale_w[...]
        for u in range(8):
            new_basis[group * 8 + u] = sketch[group * 8 + u] * scale
        return 0

    lax.fori_loop(0, 8, scaled, 0)
    copies = fetched([(new_basis, new_at)], sent)

    for tile in range(4):
        low = 8 * tile
        acc = weighted(
            8, 64, 16,
            lambda i, group, u: sketch[group * 16 + u, low + i : low + i + 1, :],
            lambda group, u: sketch[group * 16 + u, low:32, :],
            [jnp.zeros((32 - low, 128), F32)] * 8,
        )
        for i in range(8):
            a = low + i
            row = scale_w[a : a + 1, :] * (1.0 / 64)
            gram[a * 32 + low : a * 32 + 32, :] = acc[i]
            fresh[a, low:32, :] = acc[i] * row
            for b in range(0, low, 8):
                fresh[a, b : b + 8, :] = gram[pl.ds(b * 32 + a, 8, stride=32), :] * row
        ranks = pl.ds(low, 8)
        copy = pltpu.make_async_copy(fresh.at[ranks], fresh_at.at[ranks], sent.at[1 + tile])
        copy.start()
        copies.append(copy)
    for copy in copies:
        copy.wait()


def shards(
    samples, leaf_basis_matrix, transfer, leaf_lists, leaf_coupling, parent_lists,
    parent_coupling, test_matrix,
):
    basis = leaf_basis_matrix.reshape(2048, 128)
    moves = transfer.reshape(1024, 128)
    near = leaf_coupling.reshape(4096, 128)
    above = parent_coupling.reshape(4096, 64)
    vmem = pl.BlockSpec(memory_space=pltpu.VMEM)
    anywhere = pl.BlockSpec(memory_space=pl.ANY)

    coeff = pl.pallas_call(
        coeff_kernel,
        out_shape=jax.ShapeDtypeStruct((768, 128), BF16),
        in_specs=[anywhere] * 3,
        out_specs=anywhere,
        scratch_shapes=[
            pltpu.VMEM((16, 8192), BF16),
            pltpu.VMEM((2048, 128), BF16),
            pltpu.VMEM((1024, 128), BF16),
            pltpu.VMEM((256, 8, 128), F32),
            pltpu.VMEM((128, 8, 128), F32),
            pltpu.VMEM((1024, 128), F32),
            pltpu.VMEM((1024, 128), F32),
            pltpu.VMEM((32, 16, 128), F32),
            pltpu.VMEM((32, 16, 128), F32),
            pltpu.VMEM((768, 128), BF16),
            pltpu.SemaphoreType.DMA((3,)),
            pltpu.SemaphoreType.DMA((2,)),
        ],
        compiler_params=pltpu.CompilerParams(vmem_limit_bytes=62 << 20),
        name="coeff",
    )(samples, basis, moves)

    peers = lax.axis_size("cluster") * lax.axis_size("replica")
    outer = lax.ppermute(coeff, HOPS, swaps(range(1, peers - 1, 2)))
    inner = lax.ppermute(coeff, HOPS, swaps(range(0, peers - 1, 2)))

    groups = lax.axis_size("vector")
    half = groups // 2
    own, transfer_w, coupling_w, parent_w = pl.pallas_call(
        wide_kernel,
        out_shape=(
            jax.ShapeDtypeStruct((768, 128), BF16),
            jax.ShapeDtypeStruct((128, 8, 128), F32),
            jax.ShapeDtypeStruct((512, 8, 128), F32),
            jax.ShapeDtypeStruct((256, 8, 128), F32),
        ),
        in_specs=[vmem] * 4,
        out_specs=(vmem,) * 4,
        cost_estimate=pl.CostEstimate(flops=10**7, bytes_accessed=10**6, transcendentals=0),
        compiler_params=pltpu.CompilerParams(vmem_limit_bytes=24 << 20),
        name="wide",
    )(coeff, moves, near, above)

    total = pl.pallas_call(
        far_kernel,
        out_shape=jax.ShapeDtypeStruct((half, 528, 128), BF16),
        in_specs=[vmem] * 9,
        out_specs=anywhere,
        scratch_shapes=[
            pltpu.VMEM((4, 32, 16, 128), F32),
            pltpu.VMEM((32, 16, 128), F32),
            pltpu.VMEM((16, 16, 128), F32),
            pltpu.VMEM((32, 16, 128), F32),
            pltpu.VMEM((528, 128), BF16),
            pltpu.SemaphoreType.DMA((groups,)),
        ],
        compiler_params=pltpu.CompilerParams(vmem_limit_bytes=24 << 20),
        name="far",
    )(own, inner, outer, transfer_w, coupling_w, parent_w, leaf_lists, parent_lists, test_matrix)

    cores = [[2 * y + core for y in range(half)] for core in range(2)]
    mine = lax.all_to_all(total, "vector", 0, 0, tiled=True, axis_index_groups=cores)

    product = pl.pallas_call(
        product_kernel,
        out_shape=jax.ShapeDtypeStruct((16, 8192), BF16),
        in_specs=[vmem] * 2,
        out_specs=vmem,
        scratch_shapes=[
            pltpu.VMEM((256, 8, 128), F32),
            pltpu.VMEM((32, 16, 128), F32),
            pltpu.VMEM((1024, 128), F32),
            pltpu.VMEM((1024, 128), F32),
        ],
        cost_estimate=pl.CostEstimate(flops=10**7, bytes_accessed=10**6, transcendentals=0),
        compiler_params=pltpu.CompilerParams(vmem_limit_bytes=24 << 20),
        name="product",
    )(total, basis)

    mine, product = lax.optimization_barrier((mine, product))
    partial = pl.pallas_call(
        part_kernel,
        out_shape=jax.ShapeDtypeStruct((1024, 128), BF16),
        in_specs=[vmem],
        out_specs=vmem,
        cost_estimate=pl.CostEstimate(flops=10**7, bytes_accessed=10**6, transcendentals=0),
        compiler_params=pltpu.CompilerParams(vmem_limit_bytes=24 << 20),
        name="part",
    )(mine)
    theirs = lax.ppermute(partial, "vector", [(i, i ^ 1) for i in range(groups)])

    new_basis, fresh = pl.pallas_call(
        basis_kernel,
        out_shape=(
            jax.ShapeDtypeStruct((64, 32, 128), F32),
            jax.ShapeDtypeStruct((32, 32, 128), F32),
        ),
        in_specs=[vmem] * 3,
        out_specs=(anywhere, anywhere),
        scratch_shapes=[
            pltpu.VMEM((256, 8, 128), F32),
            pltpu.VMEM((32, 32, 128), F32),
            pltpu.VMEM((64, 32, 128), F32),
            pltpu.VMEM((32, 128), F32),
            pltpu.VMEM((1024, 128), F32),
            pltpu.VMEM((64, 32, 128), F32),
            pltpu.VMEM((32, 32, 128), F32),
            pltpu.SemaphoreType.DMA((5,)),
        ],
        compiler_params=pltpu.CompilerParams(vmem_limit_bytes=24 << 20),
        name="basis",
    )(partial, theirs, basis)
    return product, new_basis, fresh


def solution(mesh):
    placed = (
        P("vector", HOPS),
        P(None, None, HOPS),
        P(None, None, HOPS),
        P(None, HOPS),
        P(None, None, None, HOPS),
        P(None, HOPS),
        P(None, None, None, HOPS),
        P("vector", None),
    )
    return jax.shard_map(
        shards,
        mesh=mesh,
        in_specs=placed,
        out_specs=(P("vector", HOPS), P(None, None, HOPS), P(None, None, HOPS)),
        check_vma=False,
    )
```

```python
import jax
import jax.numpy as jnp
from jax import lax
from jax.experimental import pallas as pl
from jax.experimental.pallas import tpu as pltpu
from jax.sharding import PartitionSpec as P

F32, BF16 = jnp.float32, jnp.bfloat16
HOPS = ("cluster", "replica")


def iota(shape, dim):
    return lax.broadcasted_iota(jnp.int32, shape, dim)


def picked(mask):
    return jnp.where(mask, 1.0, 0.0).astype(BF16)


def dot(a, b, contract=((1,), (0,))):
    return lax.dot_general(a, b, (contract, ((), ())), preferred_element_type=F32)


def widen(src, dst, step=128):
    tiles = step // 8

    def body(i, _):
        rows = src[pl.ds(pl.multiple_of(i * step, step), step), :].astype(F32)
        dst[pl.ds(i * tiles, tiles)] = rows.reshape(tiles, 8, rows.shape[-1])
        return 0

    lax.fori_loop(0, src.shape[0] // step, body, 0)


def weighted(block, steps, unroll, weight, term, init):
    def body(group, acc):
        acc = list(acc)
        for u in range(unroll):
            src = term(group, u)
            for i in range(block):
                acc[i] = acc[i] + weight(i, group, u) * src
        return tuple(acc)

    return lax.fori_loop(0, steps // unroll, body, tuple(init))


def lane_product(out, left, right_of, blocks, chunks, per, tile_of, start=None, block=8, at=0):
    rows, wide = out.shape[1:]

    def outer(blk, _):
        first = [at + blk * block + i for i in range(block)]
        init = [jnp.zeros((rows, wide), F32) if start is None else start[o] for o in first]

        def weight(i, group, u):
            c = u % 8
            return left[tile_of(first[i], group * per + u // 8), c : c + 1, :]

        acc = weighted(
            block, chunks * 8, per * 8, weight,
            lambda group, u: right_of(group * per + u // 8, u % 8), init,
        )
        for i, o in enumerate(first):
            out[o] = acc[i]
        return 0

    lax.fori_loop(0, blocks, outer, 0)


def swaps(firsts):
    return [pair for i in firsts for pair in ((i, i + 1), (i + 1, i))]


def fetched(pairs, sem):
    copies = [pltpu.make_async_copy(a, b, sem.at[i]) for i, (a, b) in enumerate(pairs)]
    for copy in copies:
        copy.start()
    return copies


def coeff_kernel(
    samples_at, basis_at, transfer_at, out_at,
    samples, basis, transfer, basis_w, transfer_w, xj, points, leaf, parent, out, sem, sent,
):
    copies = fetched(
        [(samples_at, samples), (basis_at, basis), (transfer_at, transfer)], sem
    )
    vecs = samples.shape[0]
    row, col = iota((256, 256), 0), iota((256, 256), 1)
    spread = picked(
        (row // 64 % 2 == col // 128) & (col % 128 == 2 * (row % 64) + row // 128)
    )
    copies[0].wait()
    for j in range(64):
        xj[pl.ds(j * vecs, vecs), :] = samples[:, 128 * j : 128 * (j + 1)].astype(F32)
    for v in range(0, vecs, 2):
        pair = [xj[pl.ds(v + i, 64, stride=vecs), :] for i in range(2)]
        turned = jnp.concatenate(pair, axis=0).T
        both = dot(
            jnp.concatenate([turned[:64], turned[64:]], axis=1).astype(BF16), spread
        )
        for i in range(2):
            points[pl.ds(v + i, 64, stride=vecs), :] = both[:, 128 * i : 128 * (i + 1)]
    copies[1].wait()
    widen(basis, basis_w)
    lane_product(
        leaf, basis_w,
        lambda chunk, c: points[pl.ds(pl.multiple_of((chunk * 8 + c) * vecs, 16), vecs), :], 4, 8, 8,
        lambda r, chunk: r * 8 + chunk,
    )
    rounded = leaf[...].astype(BF16)
    out[0:512, :] = rounded.reshape(512, 128)
    first = pltpu.make_async_copy(out.at[0:512], out_at.at[0:512], sent.at[0])
    first.start()
    leaf[...] = rounded.astype(F32)
    copies[2].wait()
    widen(transfer, transfer_w)

    def outer(blk, _):
        acc = weighted(
            8, 32, 32,
            lambda i, group, u: transfer_w[(group * 32 + u) * 4 + blk, i : i + 1, :],
            lambda group, u: leaf[group * 32 + u],
            [jnp.zeros((vecs, 128), F32)] * 8,
        )
        for i in range(8):
            parent[blk * 8 + i] = acc[i] + pltpu.roll(acc[i], 127, 1)
        return 0

    lax.fori_loop(0, 4, outer, 0)
    low = picked(iota((128, 128), 0) == 2 * iota((128, 128), 1))
    high = picked(iota((128, 128), 0) == 2 * iota((128, 128), 1) - 128)
    sums = parent[...].reshape(512, 128).astype(BF16)
    out[512:768, :] = (dot(sums[0:256], low) + dot(sums[256:512], high)).astype(BF16)
    second = pltpu.make_async_copy(out.at[512:768], out_at.at[512:768], sent.at[1])
    second.start()
    first.wait()
    second.wait()


def wide_kernel(coeff, transfer, leaf_b, parent_b, own, transfer_w, coupling_w, parent_w):
    own[...] = coeff[...]
    widen(transfer, transfer_w)

    def pack(i, _):
        low = parent_b[pl.ds(pl.multiple_of(i * 128, 128), 128), :].astype(F32)
        high = parent_b[pl.ds(pl.multiple_of(2048 + i * 128, 128), 128), :].astype(F32)
        both = jnp.concatenate([low, high], axis=1)
        parent_w[pl.ds(i * 16, 16)] = both.reshape(16, 8, 128)
        return 0

    lax.fori_loop(0, 16, pack, 0)
    widen(leaf_b, coupling_w)


def far_kernel(
    own, inner, outer, transfer_w, coupling_w, parent_w, leaf_lists, parent_lists, test,
    out, source, far, pfar, wide, payload, sent,
):
    place = lax.axis_index("cluster") * lax.axis_size("replica") + lax.axis_index("replica")
    odd = lax.rem(place, 2) == 1

    def three(low, high):
        one, other = inner[low:high], outer[low:high]
        before, after = jnp.where(odd, one, other), jnp.where(odd, other, one)
        return jnp.concatenate([before, own[low:high], after], axis=1)

    first = place * 64 - 64
    none = jnp.zeros((64, 128), BF16)
    lists = jnp.concatenate([parent_lists[...], parent_lists[...]], axis=1) - first
    packed = three(512, 768)
    for k in range(4):
        index = jnp.broadcast_to(lists[k : k + 1, :], (64, 128))
        parts = []
        for m in range(3):
            hit = picked(iota((64, 128), 0) + 64 * m == index)
            parts += [jnp.concatenate(two, axis=1) for two in ((hit, none), (none, hit))]
        got = dot(packed, jnp.concatenate(parts, axis=0))
        for h in range(2):
            part = got[:, 128 * h : 128 * (h + 1)]
            source[k, 16 * h : 16 * (h + 1)] = part.reshape(16, 16, 128)

    lane_product(
        pfar, parent_w, lambda chunk, c: source[c % 4, chunk * 2 + c // 4], 2, 16, 8,
        lambda r, chunk: r * 16 + chunk,
    )
    lane = iota((256, 128), 1) // 2
    flat = pfar[...].reshape(256, 128)
    wide[0:16] = jnp.take_along_axis(flat, lane, axis=1).reshape(16, 16, 128)
    wide[16:32] = jnp.take_along_axis(flat, lane + 64, axis=1).reshape(16, 16, 128)

    first = place * 128 - 128
    rows = three(0, 512)
    for k in range(0, 4, 2):
        hits = [
            picked(
                iota((384, 128), 0)
                == jnp.broadcast_to(leaf_lists[k + i : k + i + 1, :] - first, (384, 128))
            )
            for i in range(2)
        ]
        got = dot(rows, jnp.concatenate(hits, axis=1))
        for i in range(2):
            source[k + i] = got[:, 128 * i : 128 * (i + 1)].reshape(32, 16, 128)
    lane_product(
        far, coupling_w, lambda chunk, c: source[c % 4, chunk * 2 + c // 4], 4, 16, 8,
        lambda r, chunk: r * 16 + chunk,
    )
    rows = jnp.concatenate([test[...].astype(F32), jnp.zeros((16, 128 - 32), F32)], axis=1)
    payload[512:528, :] = rows.astype(BF16)
    copies = []
    peers = out.shape[0]
    for h in range(2):
        lane_product(
            far, transfer_w, lambda chunk, c: wide[chunk * 8 + c], 2, 4, 4,
            lambda a, chunk: a * 4 + chunk, start=far, at=16 * h,
        )
        low = 256 * h
        payload[low : low + 256, :] = far[16 * h : 16 * (h + 1)].reshape(256, 128).astype(BF16)
        sent_rows = pl.ds(low, 256 if h == 0 else 272)
        for y in range(peers):
            copy = pltpu.make_async_copy(
                payload.at[sent_rows], out.at[y, sent_rows], sent.at[peers * h + y]
            )
            copy.start()
            copies.append(copy)
    for copy in copies:
        copy.wait()


def product_kernel(total, basis, out, basis_w, total_w, grid, turned):
    widen(basis, basis_w)
    total_w[...] = total[0, 0:512, :].astype(F32).reshape(32, 16, 128)

    def outer(blk, _):
        acc = weighted(
            8, 32, 32,
            lambda i, group, u: basis_w[(group * 32 + u) * 8 + blk, i : i + 1, :],
            lambda group, u: total_w[group * 32 + u],
            [jnp.zeros((16, 128), F32)] * 8,
        )
        for i in range(8):
            grid[pl.ds(pl.multiple_of((blk * 8 + i) * 16, 16), 16), :] = acc[i]
        return 0

    lax.fori_loop(0, 8, outer, 0)
    even = picked(iota((64, 128), 1) == 2 * iota((64, 128), 0))
    odd = picked(iota((64, 128), 1) == 2 * iota((64, 128), 0) + 1)
    none = jnp.zeros((64, 128), BF16)
    for v in range(16):
        mine = grid[pl.ds(v, 64, stride=16), :].astype(BF16)
        turned[pl.ds(v, 64, stride=16), :] = dot(even, jnp.concatenate([mine, none], axis=0), ((1,), (1,))) + dot(
            odd, jnp.concatenate([none, mine], axis=0), ((1,), (1,))
        )
    for j in range(64):
        out[:, 128 * j : 128 * (j + 1)] = turned[16 * j : 16 * (j + 1), :].astype(BF16)


def part_kernel(totals, partial):
    groups = range(totals.shape[0])
    tests = jnp.concatenate([totals[g, 512:528, :] for g in groups], axis=0)
    across = tests.astype(F32).T[0:32].astype(BF16)
    for a in range(32):
        rows = jnp.concatenate([totals[g, 16 * a : 16 * (a + 1), :] for g in groups], axis=0)
        partial[32 * a : 32 * (a + 1), :] = dot(across, rows).astype(BF16)


def basis_kernel(
    mine, theirs, basis, new_at, fresh_at,
    basis_w, compressed, sketch, scale_w, gram, new_basis, fresh, sent,
):
    widen(basis, basis_w)
    for a in range(0, 1024, 128):
        both = mine[a : a + 128, :].astype(F32) + theirs[a : a + 128, :].astype(F32)
        compressed[a // 32 : a // 32 + 4] = both.reshape(4, 32, 128)
    scale_w[...] = jnp.zeros((32, 128), F32)

    def outer(blk, _):
        acc = weighted(
            8, 32, 32,
            lambda i, group, u: basis_w[(group * 32 + u) * 8 + blk, i : i + 1, :],
            lambda group, u: compressed[group * 32 + u],
            [jnp.zeros((32, 128), F32)] * 8,
        )
        square = scale_w[...]
        for i in range(8):
            sketch[blk * 8 + i] = acc[i]
            square = square + acc[i] * acc[i]
        scale_w[...] = square
        return 0

    lax.fori_loop(0, 8, outer, 0)
    scale_w[...] = lax.rsqrt(scale_w[...] / 64 + 1e-06)

    def scaled(group, _):
        scale = scale_w[...]
        for u in range(8):
            new_basis[group * 8 + u] = sketch[group * 8 + u] * scale
        return 0

    lax.fori_loop(0, 8, scaled, 0)
    copies = fetched([(new_basis, new_at)], sent)

    for tile in range(4):
        low = 8 * tile
        acc = weighted(
            8, 64, 32,
            lambda i, group, u: sketch[group * 32 + u, low + i : low + i + 1, :],
            lambda group, u: sketch[group * 32 + u, low:32, :],
            [jnp.zeros((32 - low, 128), F32)] * 8,
        )
        for i in range(8):
            a = low + i
            row = scale_w[a : a + 1, :] * (1.0 / 64)
            gram[a * 32 + low : a * 32 + 32, :] = acc[i]
            fresh[a, low:32, :] = acc[i] * row
            for b in range(0, low, 8):
                fresh[a, b : b + 8, :] = gram[pl.ds(b * 32 + a, 8, stride=32), :] * row
        ranks = pl.ds(low, 8)
        copy = pltpu.make_async_copy(fresh.at[ranks], fresh_at.at[ranks], sent.at[1 + tile])
        copy.start()
        copies.append(copy)
    for copy in copies:
        copy.wait()


def shards(
    samples, leaf_basis_matrix, transfer, leaf_lists, leaf_coupling, parent_lists,
    parent_coupling, test_matrix,
):
    basis = leaf_basis_matrix.reshape(2048, 128)
    moves = transfer.reshape(1024, 128)
    near = leaf_coupling.reshape(4096, 128)
    above = parent_coupling.reshape(4096, 64)
    vmem = pl.BlockSpec(memory_space=pltpu.VMEM)
    anywhere = pl.BlockSpec(memory_space=pl.ANY)

    coeff = pl.pallas_call(
        coeff_kernel,
        out_shape=jax.ShapeDtypeStruct((768, 128), BF16),
        in_specs=[anywhere] * 3,
        out_specs=anywhere,
        scratch_shapes=[
            pltpu.VMEM((16, 8192), BF16),
            pltpu.VMEM((2048, 128), BF16),
            pltpu.VMEM((1024, 128), BF16),
            pltpu.VMEM((256, 8, 128), F32),
            pltpu.VMEM((128, 8, 128), F32),
            pltpu.VMEM((1024, 128), F32),
            pltpu.VMEM((1024, 128), F32),
            pltpu.VMEM((32, 16, 128), F32),
            pltpu.VMEM((32, 16, 128), F32),
            pltpu.VMEM((768, 128), BF16),
            pltpu.SemaphoreType.DMA((3,)),
            pltpu.SemaphoreType.DMA((2,)),
        ],
        compiler_params=pltpu.CompilerParams(vmem_limit_bytes=62 << 20),
        name="coeff",
    )(samples, basis, moves)

    peers = lax.axis_size("cluster") * lax.axis_size("replica")
    outer = lax.ppermute(coeff, HOPS, swaps(range(1, peers - 1, 2)))
    inner = lax.ppermute(coeff, HOPS, swaps(range(0, peers - 1, 2)))

    groups = lax.axis_size("vector")
    half = groups // 2
    own, transfer_w, coupling_w, parent_w = pl.pallas_call(
        wide_kernel,
        out_shape=(
            jax.ShapeDtypeStruct((768, 128), BF16),
            jax.ShapeDtypeStruct((128, 8, 128), F32),
            jax.ShapeDtypeStruct((512, 8, 128), F32),
            jax.ShapeDtypeStruct((256, 8, 128), F32),
        ),
        in_specs=[vmem] * 4,
        out_specs=(vmem,) * 4,
        cost_estimate=pl.CostEstimate(flops=10**7, bytes_accessed=10**6, transcendentals=0),
        compiler_params=pltpu.CompilerParams(vmem_limit_bytes=24 << 20),
        name="wide",
    )(coeff, moves, near, above)

    total = pl.pallas_call(
        far_kernel,
        out_shape=jax.ShapeDtypeStruct((half, 528, 128), BF16),
        in_specs=[vmem] * 9,
        out_specs=anywhere,
        scratch_shapes=[
            pltpu.VMEM((4, 32, 16, 128), F32),
            pltpu.VMEM((32, 16, 128), F32),
            pltpu.VMEM((16, 16, 128), F32),
            pltpu.VMEM((32, 16, 128), F32),
            pltpu.VMEM((528, 128), BF16),
            pltpu.SemaphoreType.DMA((groups,)),
        ],
        compiler_params=pltpu.CompilerParams(vmem_limit_bytes=24 << 20),
        name="far",
    )(own, inner, outer, transfer_w, coupling_w, parent_w, leaf_lists, parent_lists, test_matrix)

    cores = [[2 * y + core for y in range(half)] for core in range(2)]
    mine = lax.all_to_all(total, "vector", 0, 0, tiled=True, axis_index_groups=cores)

    product = pl.pallas_call(
        product_kernel,
        out_shape=jax.ShapeDtypeStruct((16, 8192), BF16),
        in_specs=[vmem] * 2,
        out_specs=vmem,
        scratch_shapes=[
            pltpu.VMEM((256, 8, 128), F32),
            pltpu.VMEM((32, 16, 128), F32),
            pltpu.VMEM((1024, 128), F32),
            pltpu.VMEM((1024, 128), F32),
        ],
        cost_estimate=pl.CostEstimate(flops=10**7, bytes_accessed=10**6, transcendentals=0),
        compiler_params=pltpu.CompilerParams(vmem_limit_bytes=24 << 20),
        name="product",
    )(total, basis)

    mine, product = lax.optimization_barrier((mine, product))
    partial = pl.pallas_call(
        part_kernel,
        out_shape=jax.ShapeDtypeStruct((1024, 128), BF16),
        in_specs=[vmem],
        out_specs=vmem,
        cost_estimate=pl.CostEstimate(flops=10**7, bytes_accessed=10**6, transcendentals=0),
        compiler_params=pltpu.CompilerParams(vmem_limit_bytes=24 << 20),
        name="part",
    )(mine)
    theirs = lax.ppermute(partial, "vector", [(i, i ^ 1) for i in range(groups)])

    new_basis, fresh = pl.pallas_call(
        basis_kernel,
        out_shape=(
            jax.ShapeDtypeStruct((64, 32, 128), F32),
            jax.ShapeDtypeStruct((32, 32, 128), F32),
        ),
        in_specs=[vmem] * 3,
        out_specs=(anywhere, anywhere),
        scratch_shapes=[
            pltpu.VMEM((256, 8, 128), F32),
            pltpu.VMEM((32, 32, 128), F32),
            pltpu.VMEM((64, 32, 128), F32),
            pltpu.VMEM((32, 128), F32),
            pltpu.VMEM((1024, 128), F32),
            pltpu.VMEM((64, 32, 128), F32),
            pltpu.VMEM((32, 32, 128), F32),
            pltpu.SemaphoreType.DMA((5,)),
        ],
        compiler_params=pltpu.CompilerParams(vmem_limit_bytes=24 << 20),
        name="basis",
    )(partial, theirs, basis)
    return product, new_basis, fresh


def solution(mesh):
    placed = (
        P("vector", HOPS),
        P(None, None, HOPS),
        P(None, None, HOPS),
        P(None, HOPS),
        P(None, None, None, HOPS),
        P(None, HOPS),
        P(None, None, None, HOPS),
        P("vector", None),
    )
    return jax.shard_map(
        shards,
        mesh=mesh,
        in_specs=placed,
        out_specs=(P("vector", HOPS), P(None, None, HOPS), P(None, None, HOPS)),
        check_vma=False,
    )
```
